256 devices in a mesh: ctx: 32 (over x, y, core), head: 8 (over z).
Axes of the slice: x: 4, y: 4, z: 8, core: 2. Of those that a mesh axis runs over, the one named last changes fastest.
Arguments:
- lin_q: bfloat16 [8192, 8192], P('ctx', 'head'), may hold values from -4 to 4
- lin_k: bfloat16 [8192, 8192], P('ctx', 'head'), may hold values from -4 to 4
- lin_v: bfloat16 [8192, 8192], P('ctx', 'head'), may hold values from -6 to 6
- log_decay: float32 [64, 8192], P('head', 'ctx'), may hold values from -1 to 0
- lin_gain: float32 [8192], P('head'), may hold values from 0.1 to 1.9
- soft_q: bfloat16 [8192, 8192], P(('ctx', 'head')), may hold values from -200 to 200
- soft_kv: bfloat16 [8192, 2048], P(('ctx', 'head')), may hold values from -8 to 8
Outputs:
- lin_out: bfloat16 [8192, 8192], P('ctx', 'head')
- soft_out: bfloat16 [8192, 8192], P(('ctx', 'head'))
The draws below stay inside these ranges and needn't reach their ends.
All inputs are finite; a program needn't handle non-finite values.
Results may differ from the reference program's by a relative error of at most 0.013.
Values may be sent and summed in bfloat16 or wider, within the bound.
No kernel may reach another device: no remote copies, remote signals or barrier semaphores. Data moves between devices by JAX's collectives and lax.ppermute only.
A program may use at most 64 MiB of HBM per device.

```python
import math
import jax
import jax.numpy as jnp
from jax import lax

HEAD_COUNT = 64
KVH = 8
DH = 128
BLOCK = 256
SEQUENCE_LENGTH = 8192


def draw_log_decay(key, part):
    key_matrix = jax.random.split(jax.random.fold_in(key, 7), 6)
    share = 0.5
    fast = jax.random.uniform(key_matrix[0], (HEAD_COUNT,)) < share
    fast_rate = jnp.exp(jax.random.uniform(key_matrix[1], (HEAD_COUNT,), minval=math.log(0.05), maxval=math.log(0.1)))
    slow_rate = jnp.exp(jax.random.uniform(key_matrix[2], (HEAD_COUNT,), minval=math.log(0.02), maxval=math.log(0.3))) * math.log(10.0) / SEQUENCE_LENGTH
    decay_speed = jnp.where(fast, fast_rate, slow_rate)[:, None]
    decay_factor = jnp.exp(jax.random.uniform(key_matrix[3], (HEAD_COUNT, SEQUENCE_LENGTH // BLOCK), minval=math.log(0.5), maxval=math.log(1.5)))
    decay_factor = jnp.repeat(decay_factor, BLOCK, axis=1)
    sudden_decay = jax.random.uniform(key_matrix[4], (HEAD_COUNT, SEQUENCE_LENGTH)) < 3.0 / SEQUENCE_LENGTH
    sudden_log_decay = jnp.log(jax.random.uniform(key_matrix[5], (HEAD_COUNT, SEQUENCE_LENGTH), minval=0.5, maxval=0.8))
    value_rows = -decay_speed * decay_factor + jnp.where(sudden_decay, sudden_log_decay, 0.0)
    return value_rows.astype(jnp.float32)


def soft_parts(key):
    key_matrix = jax.random.split(jax.random.fold_in(key, 11), 3)
    queries = jax.random.normal(key_matrix[0], (SEQUENCE_LENGTH, HEAD_COUNT, DH), jnp.float32)
    keyrows = jax.random.normal(key_matrix[1], (SEQUENCE_LENGTH, KVH, DH), jnp.float32)
    value_rows = jax.random.normal(key_matrix[2], (SEQUENCE_LENGTH, KVH, DH), jnp.float32)
    queries = jnp.clip(queries, -200.0, 200.0)
    keyrows = jnp.clip(keyrows, -8.0, 8.0)
    value_rows = jnp.clip(value_rows, -8.0, 8.0)
    joined = jnp.stack([keyrows, value_rows], axis=2).reshape(SEQUENCE_LENGTH, KVH * 2 * DH)
    return (queries.reshape(SEQUENCE_LENGTH, HEAD_COUNT * DH), joined)


def draw_soft_q(key, part):
    queries, joined = soft_parts(key)
    return queries.astype(jnp.bfloat16)


def draw_soft_kv(key, part):
    queries, joined = soft_parts(key)
    return joined.astype(jnp.bfloat16)


def block_scale(stream_key, dims, shards, low, top_value):
    gain, own = 1.0, jax.random.fold_in(stream_key, 6)
    for position, blocks in shards:
        draws = jnp.exp(jax.random.uniform(jax.random.fold_in(own, position), (blocks,), jnp.float32, low / len(shards), top_value / len(shards)))
        gain = gain * jnp.repeat(draws, dims[position] // blocks).reshape([-1 if axis == position else 1 for axis in range(len(dims))])
    return gain


def gaussian(rng, extent, scale, reach, cuts=(), dtype=jnp.bfloat16):
    entries = jax.random.normal(rng, extent, jnp.float32) * scale
    if len(cuts) > 0:
        entries = block_scale(rng, extent, cuts, -0.22, 0.18) * entries
    return jnp.clip(entries, min=-reach, max=reach).astype(dtype)


def setup_inputs(seed: int = 0) -> dict:
    arg_keys = jax.random.split(jax.random.key(seed), 8)
    return {
        "lin_q": gaussian(arg_keys[0], (SEQUENCE_LENGTH, HEAD_COUNT * DH), 0.3, 4.0, ((0, 32), (1, 8))),
        "lin_k": gaussian(arg_keys[1], (SEQUENCE_LENGTH, HEAD_COUNT * DH), 0.3, 4.0, ((0, 32), (1, 8))),
        "lin_v": gaussian(arg_keys[2], (SEQUENCE_LENGTH, HEAD_COUNT * DH), 1.0, 6.0, ((0, 32), (1, 8))),
        "log_decay": draw_log_decay(jax.random.fold_in(arg_keys[7], 71), 0),
        "lin_gain": jnp.clip(1.0 + 0.18 * jax.random.normal(arg_keys[4], (HEAD_COUNT * DH,), jnp.float32), 0.1, 1.9),
        "soft_q": draw_soft_q(jax.random.fold_in(arg_keys[7], 71), 0),
        "soft_kv": draw_soft_kv(jax.random.fold_in(arg_keys[7], 71), 0),
    }


def rounded(x):
    return lax.optimization_barrier(x.astype(jnp.bfloat16)).astype(jnp.float32)

def block_terms(qb, kb, vb, gb, state):
    size = gb.shape[1]
    cum = jnp.cumsum(gb, axis=1)
    pos = jnp.arange(size)
    causal = pos[:, None] >= pos[None, :]
    diff = cum[:, :, None] - cum[:, None, :]
    weight = jnp.where(causal[None], jnp.exp(jnp.minimum(diff, 0.0)), 0.0)
    qf = qb.astype(jnp.float32)
    kf = kb.astype(jnp.float32)
    vf = vb.astype(jnp.float32)
    scores = jnp.einsum('thd,shd->hts', qf, kf)
    probs = rounded(scores * weight)
    intra = jnp.einsum('hts,shd->thd', probs, vf)
    inter = jnp.exp(cum).T[:, :, None] * jnp.einsum('thd,hde->the', qf, rounded(state))
    keys_scaled = rounded(kf * jnp.exp(cum[:, -1:] - cum).T[:, :, None])
    local = jnp.einsum('shd,she->hde', keys_scaled, vf)
    return (intra + inter, local, cum[:, -1])

def lightning_layer(lin_q, lin_k, lin_v, log_decay, lin_gain):
    nblk = SEQUENCE_LENGTH // BLOCK
    q = lin_q.reshape(nblk, BLOCK, HEAD_COUNT, DH)
    k = lin_k.reshape(nblk, BLOCK, HEAD_COUNT, DH)
    v = lin_v.reshape(nblk, BLOCK, HEAD_COUNT, DH)
    g = log_decay.reshape(HEAD_COUNT, nblk, BLOCK).transpose(1, 0, 2)

    def advance(state, xs):
        qb, kb, vb, gb = xs
        mixed, local, total = block_terms(qb, kb, vb, gb, state)
        state = jnp.exp(total)[:, None, None] * state + local
        return (state, mixed)
    init = jnp.zeros((HEAD_COUNT, DH, DH), jnp.float32)
    final, mixed = lax.scan(advance, init, (q, k, v, g))
    rms = jnp.sqrt(lax.optimization_barrier(jnp.mean(mixed * mixed, axis=-1, keepdims=True)) + 1e-05)
    normed = mixed / rms * lin_gain.reshape(HEAD_COUNT, DH)
    return normed.reshape(SEQUENCE_LENGTH, HEAD_COUNT * DH).astype(jnp.bfloat16)

def softmax_layer(soft_q, soft_kv):
    group = HEAD_COUNT // KVH
    q = soft_q.reshape(SEQUENCE_LENGTH, KVH, group, DH)
    kv = soft_kv.reshape(SEQUENCE_LENGTH, KVH, 2, DH)
    qblock = 256 if SEQUENCE_LENGTH % 256 == 0 else SEQUENCE_LENGTH
    nq = SEQUENCE_LENGTH // qblock
    scale = DH ** (-0.5)
    kpos = jnp.arange(SEQUENCE_LENGTH)

    def one_head(index):
        qn = lax.dynamic_index_in_dim(q, index, 1, keepdims=False).astype(jnp.float32)
        kvn = lax.dynamic_index_in_dim(kv, index, 1, keepdims=False).astype(jnp.float32)
        key_matrix = kvn[:, 0]
        value_rows = kvn[:, 1]

        def one_block(bidx):
            qblk = lax.dynamic_slice_in_dim(qn, bidx * qblock, qblock, 0)
            qpos = bidx * qblock + jnp.arange(qblock)
            scores = jnp.einsum('qgd,kd->gqk', qblk, key_matrix) * scale
            mask = kpos[None, :] <= qpos[:, None]
            scores = jnp.where(mask[None], scores, -jnp.inf)
            peak = lax.optimization_barrier(jnp.max(scores, axis=-1, keepdims=True))
            weights = jnp.where(mask[None], jnp.exp(scores - peak), 0.0)
            denom = lax.optimization_barrier(jnp.sum(weights, axis=-1))
            out = jnp.einsum('gqk,kd->gqd', rounded(weights), value_rows) / denom[:, :, None]
            return out.transpose(1, 0, 2)
        outs = lax.map(one_block, jnp.arange(nq))
        return outs.reshape(SEQUENCE_LENGTH, group, DH)
    heads = lax.map(one_head, jnp.arange(KVH))
    return heads.transpose(1, 0, 2, 3).reshape(SEQUENCE_LENGTH, HEAD_COUNT * DH).astype(jnp.bfloat16)

def reference(lin_q, lin_k, lin_v, log_decay, lin_gain, soft_q, soft_kv):
    lin_out = lightning_layer(lin_q, lin_k, lin_v, log_decay, lin_gain)
    soft_out = softmax_layer(soft_q, soft_kv)
    return (lin_out, soft_out)
```

```python
import functools
import math

import jax
import jax.numpy as jnp
from jax import lax
from jax.experimental import pallas as pl
from jax.experimental.pallas import tpu as pltpu
from jax.sharding import Mesh
from jax.sharding import PartitionSpec as P

CTX = ("ctx_0", "ctx_1", "ctx_2")
CTX_HEAD = ("ctx_0", "ctx_1", "ctx_2", "head")
NX, NY, NC, NZ = 4, 4, 2, 8
CH = 256
DIM = 128
HEADS = 8
MSG = 48

NT = (((1,), (1,)), ((), ()))
NN = (((1,), (0,)), ((), ()))
TN = (((0,), (0,)), ((), ()))


def dot(a, b, dims):
    return lax.dot_general(a, b, dims, preferred_element_type=jnp.float32)


def running_sum(g):
    lane = lax.broadcasted_iota(jnp.int32, g.shape, 1)
    step = 1
    while step < g.shape[1]:
        g = g + jnp.where(lane >= step, pltpu.roll(g, step, 1), 0.0)
        step *= 2
    return g


def columns(cum):
    wide = jnp.concatenate([cum, jnp.zeros((DIM - cum.shape[0], cum.shape[1]), cum.dtype)], 0)
    return wide.T


def local_state_kernel(k_ref, v_ref, g_ref, msg_ref):
    cum = running_sum(g_ref[...])
    cum_t = columns(cum)
    row = lax.broadcasted_iota(jnp.int32, (16, DIM), 0)
    for h in range(HEADS):
        cols = slice(h * DIM, (h + 1) * DIM)
        last = cum[h : h + 1, CH - 1 : CH]
        scale = jnp.exp(last - cum_t[:, h : h + 1])
        ks = (k_ref[:, cols].astype(jnp.float32) * scale).astype(jnp.bfloat16)
        local = dot(ks, v_ref[:, cols], TN).astype(jnp.bfloat16)
        total = jnp.broadcast_to(last, (16, DIM))
        hi = total.astype(jnp.bfloat16).astype(jnp.float32)
        extra = jnp.where(row == 0, hi, jnp.where(row == 1, total - hi, 0.0)).astype(jnp.bfloat16)
        for piece in range(4):
            msg_ref[h * 4 + piece, 0:32, :] = local[piece * 32 : (piece + 1) * 32]
            msg_ref[h * 4 + piece, 32:48, :] = extra


def scan_kernel(msg_ref, out_ref):
    state = jnp.zeros((32, DIM), jnp.float32)
    for j in range(msg_ref.shape[0]):
        out_ref[j] = state.astype(jnp.bfloat16)
        extra = msg_ref[j, 32:48, :].astype(jnp.float32)
        decay = jnp.exp(extra[0:1] + extra[1:2])
        state = decay * state + msg_ref[j, 0:32, :].astype(jnp.float32)


def lightning_kernel(q_ref, k_ref, v_ref, g_ref, gain_ref, state_ref, out_ref):
    cum = running_sum(g_ref[...])
    cum_t = columns(cum)
    causal = lax.broadcasted_iota(jnp.int32, (CH, CH), 0) >= lax.broadcasted_iota(
        jnp.int32, (CH, CH), 1
    )
    for h in range(HEADS):
        cols = slice(h * DIM, (h + 1) * DIM)
        q, k, v = q_ref[:, cols], k_ref[:, cols], v_ref[:, cols]
        col = cum_t[:, h : h + 1]
        diff = jnp.minimum(col - cum[h : h + 1, :], 0.0)
        weight = jnp.where(causal, jnp.exp(diff), 0.0)
        probs = (dot(q, k, NT) * weight).astype(jnp.bfloat16)
        mix = dot(probs, v, NN) + jnp.exp(col) * dot(q, state_ref[h], NN)
        norm = lax.rsqrt(jnp.mean(mix * mix, axis=1, keepdims=True) + 1e-05)
        out_ref[:, cols] = (mix * norm * gain_ref[:, cols]).astype(jnp.bfloat16)


ROWS = HEADS * 64
SUB = 128
KEYS = 1024


def softmax_kernel(*refs):
    q_ref = refs[0]
    pieces = refs[1:11]
    out_ref, kv_ref, qq_ref, m_ref, acc_ref, sems = refs[11:]
    mx, my, mc = (lax.axis_index(a) for a in CTX)

    copies = []
    for other in range(2):
        row, plus, minus, far_a, far_b = pieces[5 * other : 5 * other + 5]
        core = mc if other == 0 else 1 - mc
        for ds, source in ((0, row), (1, plus), (3, minus), (2, None)):
            for slot, df in enumerate((0, 1, 3, 2)):
                ref = source
                at = slot
                if source is None:
                    ref, at = (far_a, slot) if slot < 2 else (far_b, slot - 2)
                dx = jnp.where(core == 0, df, ds)
                dy = jnp.where(core == 0, ds, df)
                chunk = ((mx + NX - dx) % NX * NY + (my + NY - dy) % NY) * NC + core
                n = len(copies)
                copy = pltpu.make_async_copy(
                    ref.at[pl.ds(at * CH, CH), :],
                    kv_ref.at[pl.ds(pl.multiple_of(chunk * CH, CH), CH), :],
                    sems.at[n],
                )
                copy.start()
                copies.append(copy)

    scale = math.log2(math.e) / math.sqrt(DIM)
    for x in range(NX):
        for g in range(HEADS):
            q = q_ref[x * 64 : (x + 1) * 64, g * DIM : (g + 1) * DIM].astype(jnp.float32) * scale
            high = q.astype(jnp.bfloat16)
            low = (q - high.astype(jnp.float32)).astype(jnp.bfloat16)
            rows = slice(x * ROWS + g * 64, x * ROWS + (g + 1) * 64)
            qq_ref[rows, 0:DIM] = high
            qq_ref[rows, DIM : 2 * DIM] = low
    for copy in copies:
        copy.wait()

    yc = my * NC + mc

    def step(x, start, masked, first):
        keys = kv_ref[pl.ds(pl.multiple_of(start, KEYS), KEYS), 0:DIM]
        values = kv_ref[pl.ds(pl.multiple_of(start, KEYS), KEYS), DIM : 2 * DIM]
        keys2 = jnp.concatenate([keys, keys], axis=1)
        values2 = jnp.concatenate([values, jnp.ones_like(values)], axis=1)
        for sub in range(ROWS // SUB):
            rows = slice(sub * SUB, (sub + 1) * SUB)
            qq = qq_ref[pl.ds(pl.multiple_of(x * ROWS + sub * SUB, SUB), SUB), :]
            s = dot(qq, keys2, NT)
            if masked:
                r = lax.broadcasted_iota(jnp.int32, (SUB, 1), 0) % 64
                pos = (x * 8 + yc) * CH + (r // 8) * 32 + mx * 8 + r % 8 - start
                s = jnp.where(lax.broadcasted_iota(jnp.int32, s.shape, 1) <= pos, s, -1e30)
            peak = jnp.max(s, axis=1, keepdims=True)
            if first:
                p = jnp.exp2(s - peak).astype(jnp.bfloat16)
                acc_ref[rows, :] = dot(p, values2, NN)
                m_ref[rows, :] = jnp.broadcast_to(peak, (SUB, DIM))
            else:
                old = m_ref[rows, 0:1]
                new = jnp.maximum(old, peak)
                p = jnp.exp2(s - new).astype(jnp.bfloat16)
                alpha = jnp.exp2(old - new)
                acc_ref[rows, :] = acc_ref[rows, :] * alpha + dot(p, values2, NN)
                m_ref[rows, :] = jnp.broadcast_to(new, (SUB, DIM))

    @pl.loop(0, NX)
    def _(x):
        step(x, x * 2048, True, True)
        step(x, x * 2048 + KEYS, True, False)

        @pl.loop(0, x * (2048 // KEYS))
        def _(i):
            step(x, i * KEYS, False, False)

        for g in range(HEADS):
            rows = slice(g * 64, (g + 1) * 64)
            o = acc_ref[rows, 0:DIM] / acc_ref[rows, DIM : 2 * DIM]
            out_ref[pl.ds(pl.multiple_of(x * 64, 64), 64), g * DIM : (g + 1) * DIM] = o.astype(
                jnp.bfloat16
            )


def vmem(n):
    return [pl.BlockSpec(memory_space=pltpu.VMEM)] * n


def call(kernel, shape, dtype, n, name, flops, **kw):
    return pl.pallas_call(
        kernel,
        out_shape=jax.ShapeDtypeStruct(shape, dtype),
        in_specs=kw.pop("in_specs", vmem(n)),
        out_specs=pl.BlockSpec(memory_space=pltpu.VMEM),
        compiler_params=pltpu.CompilerParams(vmem_limit_bytes=kw.pop("limit", 32 << 20)),
        cost_estimate=pl.CostEstimate(flops=flops, bytes_accessed=2 << 20, transcendentals=0),
        name=name,
        **kw,
    )


def ctx_index(x, y, c):
    return (x % NX * NY + y % NY) * NC + c


def ring(first, sign):
    pairs = []
    for x in range(NX):
        for y in range(NY):
            for c in range(NC):
                along_x = (c == 0) == first
                to = (x + sign, y) if along_x else (x, y + sign)
                pairs.append((ctx_index(x, y, c), ctx_index(*to, c)))
    return pairs


def gather_kv(own):
    half = CH // 2
    r1 = lax.ppermute(own, CTX, ring(True, 1))
    r2 = lax.ppermute(own, CTX, ring(True, -1))
    h1 = lax.ppermute(r1[:half], CTX, ring(True, 1))
    h2 = lax.ppermute(r2[half:], CTX, ring(True, -1))
    row = jnp.concatenate([own, r1, r2, h1, h2], axis=0)
    s1 = lax.ppermute(row, CTX, ring(False, 1))
    s2 = lax.ppermute(row, CTX, ring(False, -1))
    t1 = lax.ppermute(s1[: 2 * CH], CTX, ring(False, 1))
    t2 = lax.ppermute(s2[2 * CH :], CTX, ring(False, -1))
    mine = [row, s1, s2, t1, t2]
    return mine + [lax.ppermute(p, "ctx_2", [(0, 1), (1, 0)]) for p in mine]


def body(lin_q, lin_k, lin_v, log_decay, lin_gain, soft_q, soft_kv):
    kv = lax.all_to_all(
        soft_kv.reshape(32, NZ, 2 * DIM).swapaxes(0, 1), "head", 0, 0, tiled=True
    ).reshape(CH, 2 * DIM)
    q = soft_q.reshape(NX, 8, NZ, HEADS * DIM).swapaxes(1, 2).reshape(NX * NZ, 8, HEADS * DIM)
    q = lax.all_to_all(q, ("ctx_0", "head"), 0, 0, tiled=True).reshape(CH, HEADS * DIM)

    msg = call(local_state_kernel, (32, MSG, DIM), jnp.bfloat16, 3, "local_state", 1 << 28)(
        lin_k, lin_v, log_decay
    )
    msg = lax.all_to_all(msg, CTX, 0, 0, tiled=True)
    state = call(scan_kernel, (32, 32, DIM), jnp.bfloat16, 1, "scan_state", 1 << 20)(msg)
    state = lax.all_to_all(state, CTX, 0, 0, tiled=True).reshape(HEADS, DIM, DIM)

    pieces = gather_kv(kv)
    soft = call(
        softmax_kernel,
        (CH, HEADS * DIM),
        jnp.bfloat16,
        11,
        "softmax",
        1 << 34,
        in_specs=vmem(1) + [pl.BlockSpec(memory_space=pl.ANY)] * 10,
        scratch_shapes=[
            pltpu.VMEM((NX * NY * NC * CH, 2 * DIM), jnp.bfloat16),
            pltpu.VMEM((NX * ROWS, 2 * DIM), jnp.bfloat16),
            pltpu.VMEM((ROWS, DIM), jnp.float32),
            pltpu.VMEM((ROWS, 2 * DIM), jnp.float32),
            pltpu.SemaphoreType.DMA((32,)),
        ],
    )(q, *pieces)
    soft = lax.all_to_all(
        soft.reshape(NX * NZ, 8, HEADS * DIM), ("ctx_0", "head"), 0, 0, tiled=True
    )
    soft_out = soft.reshape(NX, NZ, 8, HEADS * DIM).swapaxes(1, 2).reshape(32, NZ * HEADS * DIM)

    lin_out = call(lightning_kernel, (CH, HEADS * DIM), jnp.bfloat16, 6, "lightning", 1 << 29)(
        lin_q, lin_k, lin_v, log_decay, lin_gain.reshape(1, -1), state
    )
    return (lin_out, soft_out)


def solution(mesh):
    finer = Mesh(
        mesh.devices.reshape(NX, NY, NC, NZ), ("ctx_0", "ctx_1", "ctx_2", "head")
    )
    placed = (
        P(CTX, "head"),
        P(CTX, "head"),
        P(CTX, "head"),
        P("head", CTX),
        P("head"),
        P(CTX_HEAD, None),
        P(CTX_HEAD, None),
    )
    return jax.shard_map(
        body,
        mesh=finer,
        in_specs=placed,
        out_specs=(P(CTX, "head"), P(CTX_HEAD, None)),
        check_vma=False,
    )
```

```python
import math

import jax
import jax.numpy as jnp
from jax import lax
from jax.experimental import pallas as pl
from jax.experimental.pallas import tpu as pltpu
from jax.sharding import Mesh
from jax.sharding import PartitionSpec as P

CTX = ("ctx_0", "ctx_1", "ctx_2")
CTX_HEAD = ("ctx_0", "ctx_1", "ctx_2", "head")
NX, NY, NC, NZ = 4, 4, 2, 8
CH = 256
DIM = 128
HEADS = 8
MSG = 48

NT = (((1,), (1,)), ((), ()))
NN = (((1,), (0,)), ((), ()))
TN = (((0,), (0,)), ((), ()))


def dot(a, b, dims):
    return lax.dot_general(a, b, dims, preferred_element_type=jnp.float32)


def running_sum(g):
    lane = lax.broadcasted_iota(jnp.int32, g.shape, 1)
    step = 1
    while step < g.shape[1]:
        g = g + jnp.where(lane >= step, pltpu.roll(g, step, 1), 0.0)
        step *= 2
    return g


def columns(cum):
    wide = jnp.concatenate([cum, jnp.zeros((DIM - cum.shape[0], cum.shape[1]), cum.dtype)], 0)
    return wide.T


def local_state_kernel(k_ref, v_ref, g_ref, msg_ref):
    cum = running_sum(g_ref[...])
    cum_t = columns(cum)
    row = lax.broadcasted_iota(jnp.int32, (16, DIM), 0)
    for h in range(HEADS):
        cols = slice(h * DIM, (h + 1) * DIM)
        last = cum[h : h + 1, CH - 1 : CH]
        scale = jnp.exp(last - cum_t[:, h : h + 1])
        ks = (k_ref[:, cols].astype(jnp.float32) * scale).astype(jnp.bfloat16)
        local = dot(ks, v_ref[:, cols], TN).astype(jnp.bfloat16)
        total = jnp.broadcast_to(last, (16, DIM))
        hi = total.astype(jnp.bfloat16).astype(jnp.float32)
        extra = jnp.where(row == 0, hi, jnp.where(row == 1, total - hi, 0.0)).astype(jnp.bfloat16)
        for piece in range(4):
            msg_ref[h * 4 + piece, 0:32, :] = local[piece * 32 : (piece + 1) * 32]
            msg_ref[h * 4 + piece, 32:48, :] = extra


def scan_kernel(msg_ref, out_ref):
    state = jnp.zeros((32, DIM), jnp.float32)
    for j in range(msg_ref.shape[0]):
        out_ref[j] = state.astype(jnp.bfloat16)
        extra = msg_ref[j, 32:48, :].astype(jnp.float32)
        decay = jnp.exp(extra[0:1] + extra[1:2])
        state = decay * state + msg_ref[j, 0:32, :].astype(jnp.float32)


def lightning_kernel(q_ref, k_ref, v_ref, g_ref, gain_ref, state_ref, out_ref):
    cum = running_sum(g_ref[...])
    cum_t = columns(cum)
    causal = lax.broadcasted_iota(jnp.int32, (CH, CH), 0) >= lax.broadcasted_iota(
        jnp.int32, (CH, CH), 1
    )
    for h in range(HEADS):
        cols = slice(h * DIM, (h + 1) * DIM)
        q, k, v = q_ref[:, cols], k_ref[:, cols], v_ref[:, cols]
        col = cum_t[:, h : h + 1]
        diff = jnp.minimum(col - cum[h : h + 1, :], 0.0)
        weight = jnp.where(causal, jnp.exp(diff), 0.0)
        probs = (dot(q, k, NT) * weight).astype(jnp.bfloat16)
        mix = dot(probs, v, NN) + jnp.exp(col) * dot(q, state_ref[h], NN)
        norm = lax.rsqrt(jnp.mean(mix * mix, axis=1, keepdims=True) + 1e-05)
        out_ref[:, cols] = (mix * norm * gain_ref[:, cols]).astype(jnp.bfloat16)


ROWS = HEADS * 64
KEYS = NY * NC * CH
SCALE = math.log2(math.e) / math.sqrt(DIM)


def softmax_kernel(*refs):
    q_ref = refs[0]
    pieces = refs[1:11]
    out_ref, kv_ref, qq_ref, s_ref, p_ref, pm_ref, al_ref, m_ref, acc_ref, sems = refs[11:]
    mx, my, mc = (lax.axis_index(a) for a in CTX)
    yc = my * NC + mc

    copies = []
    for other in range(2):
        row, plus, minus, far_a, far_b = pieces[5 * other : 5 * other + 5]
        core = mc if other == 0 else 1 - mc
        for ds, source in ((0, row), (1, plus), (3, minus), (2, None)):
            for slot, df in enumerate((0, 1, 3, 2)):
                ref = source
                at = slot
                if source is None:
                    ref, at = (far_a, slot) if slot < 2 else (far_b, slot - 2)
                dx = jnp.where(core == 0, df, ds)
                dy = jnp.where(core == 0, ds, df)
                chunk = ((mx + NX - dx) % NX * NY + (my + NY - dy) % NY) * NC + core
                n = len(copies)
                copy = pltpu.make_async_copy(
                    ref.at[pl.ds(at * CH, CH), :],
                    kv_ref.at[pl.ds(pl.multiple_of(chunk * CH, CH), CH), :],
                    sems.at[n],
                )
                copy.start()
                copies.append(copy)

    for x in range(NX):
        for g in range(HEADS):
            rows = slice(x * ROWS + g * 64, x * ROWS + (g + 1) * 64)
            qq_ref[rows, :] = q_ref[x * 64 : (x + 1) * 64, g * DIM : (g + 1) * DIM]
    acc_ref[...] = jnp.zeros_like(acc_ref)
    for copy in copies:
        copy.wait()

    tiles = NX * (NX + 1) // 2

    def tile(t):
        t = jnp.int32(t)
        x = sum((t >= n).astype(jnp.int32) for n in (1, 3, 6))
        u = t - x * (x + 1) // 2
        return x, u, jnp.where(u == 0, x, u - 1) * KEYS, t % 2

    def scores(t):
        x, _, start, slot = tile(t)
        r = lax.broadcasted_iota(jnp.int32, (ROWS, 1), 0) % 64
        pos = (x * 8 + yc) * CH + (r // 8) * 32 + mx * 8 + r % 8 - start
        qq = qq_ref[pl.ds(pl.multiple_of(x * ROWS, ROWS), ROWS), :]
        for k in range(KEYS // 256):
            keys = kv_ref[pl.ds(pl.multiple_of(start + k * 256, 256), 256), 0:DIM]
            s = dot(qq, keys, NT) * SCALE
            lane = lax.broadcasted_iota(jnp.int32, s.shape, 1)
            s = jnp.where(lane <= pos - k * 256, s, -1e30)
            s_ref[slot, :, k * 256 : (k + 1) * 256] = s
            peak = jnp.maximum(s[:, :DIM], s[:, DIM:])
            if k > 0:
                peak = jnp.maximum(peak, pm_ref[slot])
            if k == KEYS // 256 - 1:
                peak = jnp.broadcast_to(jnp.max(peak, axis=1, keepdims=True), (ROWS, DIM))
            pm_ref[slot] = peak

    def weights(t):
        _, u, _, slot = tile(t)
        for i in range(ROWS // 64):
            rows = slice(i * 64, (i + 1) * 64)
            old = jnp.where(u == 0, -1e30, m_ref[rows, :])
            new = jnp.maximum(old, pm_ref[slot, rows, :])
            al_ref[slot, rows, :] = jnp.exp2(old - new)
            m_ref[rows, :] = new
            for k in range(KEYS // DIM):
                cols = slice(k * DIM, (k + 1) * DIM)
                p_ref[slot, rows, cols] = jnp.exp2(s_ref[slot, rows, cols] - new).astype(
                    jnp.bfloat16
                )

    def mix(t):
        _, _, start, slot = tile(t)
        values = kv_ref[pl.ds(pl.multiple_of(start, KEYS), KEYS), DIM : 2 * DIM]
        values = jnp.concatenate([values, jnp.ones_like(values)], axis=1)
        alpha = al_ref[slot]
        alpha = jnp.concatenate([alpha, alpha], axis=1)
        acc_ref[...] = acc_ref[...] * alpha + dot(p_ref[slot], values, NN)

    def finish(t):
        x, u, _, _ = tile(t)

        @pl.when(u == x)
        def _():
            for g in range(HEADS):
                rows = slice(g * 64, (g + 1) * 64)
                o = acc_ref[rows, 0:DIM] / acc_ref[rows, DIM : 2 * DIM]
                out_ref[pl.ds(pl.multiple_of(x * 64, 64), 64), g * DIM : (g + 1) * DIM] = o.astype(
                    jnp.bfloat16
                )

    scores(0)
    weights(0)
    scores(1)

    @pl.loop(0, tiles - 2)
    def _(t):
        mix(t)
        scores(t + 2)
        weights(t + 1)
        finish(t)

    mix(tiles - 2)
    weights(tiles - 1)
    mix(tiles - 1)
    finish(tiles - 1)


def vmem(n):
    return [pl.BlockSpec(memory_space=pltpu.VMEM)] * n


def call(kernel, shape, dtype, n, flops, **kw):
    return pl.pallas_call(
        kernel,
        out_shape=jax.ShapeDtypeStruct(shape, dtype),
        in_specs=kw.pop("in_specs", vmem(n)),
        out_specs=pl.BlockSpec(memory_space=pltpu.VMEM),
        compiler_params=pltpu.CompilerParams(vmem_limit_bytes=kw.pop("limit", 32 << 20)),
        cost_estimate=pl.CostEstimate(flops=flops, bytes_accessed=2 << 20, transcendentals=0),
        **kw,
    )


def ctx_index(x, y, c):
    return (x % NX * NY + y % NY) * NC + c


def ring(first, sign):
    pairs = []
    for x in range(NX):
        for y in range(NY):
            for c in range(NC):
                along_x = (c == 0) == first
                to = (x + sign, y) if along_x else (x, y + sign)
                pairs.append((ctx_index(x, y, c), ctx_index(*to, c)))
    return pairs


def permute(value, pairs, axes=CTX):
    return lax.ppermute(value, axes, pairs)


def exchange(value, axes):
    return lax.all_to_all(value, axes, 0, 0, tiled=True)


def gather_kv(own):
    r1 = permute(own, ring(True, 1))
    r2 = permute(own, ring(True, -1))
    r3 = permute(own, ring(True, 2))
    row = jnp.concatenate([own, r1, r2, r3], axis=0)
    s1 = permute(row, ring(False, 1))
    s2 = permute(row, ring(False, -1))
    t1 = permute(s1[: 2 * CH], ring(False, 1))
    t2 = permute(s2[2 * CH :], ring(False, -1))
    mine = [row, s1, s2, t1, t2]
    swap = [(0, 1), (1, 0)]
    return mine + [permute(p, swap, "ctx_2") for p in mine]


def both(lin_q, lin_k, lin_v, log_decay, lin_gain, soft_q, soft_kv):
    kv = soft_kv.reshape(32, NZ, 2 * DIM).swapaxes(0, 1)
    kv = exchange(kv, "head").reshape(CH, 2 * DIM)
    q = soft_q.reshape(NX, 8, NZ, HEADS * DIM).swapaxes(1, 2).reshape(NX * NZ, 8, HEADS * DIM)
    q = exchange(q, ("ctx_0", "head")).reshape(CH, HEADS * DIM)
    pieces = gather_kv(kv)

    msg = call(local_state_kernel, (32, MSG, DIM), jnp.bfloat16, 3, 1 << 28)(
        lin_k, lin_v, log_decay
    )
    msg = exchange(msg, CTX)
    state = call(scan_kernel, (32, 32, DIM), jnp.bfloat16, 1, 1 << 20)(msg)
    state = exchange(state, CTX).reshape(HEADS, DIM, DIM)

    soft = call(
        softmax_kernel,
        (CH, HEADS * DIM),
        jnp.bfloat16,
        11,
        1 << 34,
        in_specs=vmem(1) + [pl.BlockSpec(memory_space=pl.ANY)] * 10,
        limit=28 << 20,
        scratch_shapes=[
            pltpu.VMEM((NX * NY * NC * CH, 2 * DIM), jnp.bfloat16),
            pltpu.VMEM((NX * ROWS, DIM), jnp.bfloat16),
            pltpu.VMEM((2, ROWS, KEYS), jnp.float32),
            pltpu.VMEM((2, ROWS, KEYS), jnp.bfloat16),
            pltpu.VMEM((2, ROWS, DIM), jnp.float32),
            pltpu.VMEM((2, ROWS, DIM), jnp.float32),
            pltpu.VMEM((ROWS, DIM), jnp.float32),
            pltpu.VMEM((ROWS, 2 * DIM), jnp.float32),
            pltpu.SemaphoreType.DMA((32,)),
        ],
    )(q, *pieces)
    soft = exchange(soft.reshape(NX * NZ, 8, HEADS * DIM), ("ctx_0", "head"))
    soft_out = soft.reshape(NX, NZ, 8, HEADS * DIM).swapaxes(1, 2).reshape(32, NZ * HEADS * DIM)

    lin_out = call(lightning_kernel, (CH, HEADS * DIM), jnp.bfloat16, 6, 1 << 29)(
        lin_q, lin_k, lin_v, log_decay, lin_gain.reshape(1, -1), state
    )
    return (lin_out, soft_out)


def solution(mesh):
    finer = Mesh(
        mesh.devices.reshape(NX, NY, NC, NZ), ("ctx_0", "ctx_1", "ctx_2", "head")
    )
    placed = (
        P(CTX, "head"),
        P(CTX, "head"),
        P(CTX, "head"),
        P("head", CTX),
        P("head"),
        P(CTX_HEAD, None),
        P(CTX_HEAD, None),
    )
    return jax.shard_map(
        both,
        mesh=finer,
        in_specs=placed,
        out_specs=(P(CTX, "head"), P(CTX_HEAD, None)),
        check_vma=False,
    )
```

```python
import functools
import math

import jax
import jax.numpy as jnp
from jax import lax
from jax.experimental import pallas as pl
from jax.experimental.pallas import tpu as pltpu
from jax.sharding import Mesh
from jax.sharding import PartitionSpec as P

CTX = ("ctx_0", "ctx_1", "ctx_2")
CTX_HEAD = ("ctx_0", "ctx_1", "ctx_2", "head")
NX, NY, NC, NZ = 4, 4, 2, 8
CH = 256
DIM = 128
HEADS = 8
HALF = HEADS // 2
TOTAL = 16

NT = (((1,), (1,)), ((), ()))
NN = (((1,), (0,)), ((), ()))
TN = (((0,), (0,)), ((), ()))


def dot(a, b, dims):
    return lax.dot_general(a, b, dims, preferred_element_type=jnp.float32)


def running_sum(g):
    lane = lax.broadcasted_iota(jnp.int32, g.shape, 1)
    step = 1
    while step < g.shape[1]:
        g = g + jnp.where(lane >= step, pltpu.roll(g, step, 1), 0.0)
        step *= 2
    return g


def columns(cum):
    wide = jnp.concatenate([cum, jnp.zeros((DIM - cum.shape[0], cum.shape[1]), cum.dtype)], 0)
    return wide.T


def total_rows(total):
    row = lax.broadcasted_iota(jnp.int32, (TOTAL, DIM), 0)
    total = jnp.broadcast_to(total, (TOTAL, DIM))
    high = total.astype(jnp.bfloat16).astype(jnp.float32)
    return jnp.where(row == 0, high, jnp.where(row == 1, total - high, 0.0)).astype(jnp.bfloat16)


def read_total(ref, h):
    rows = ref[h, DIM : DIM + TOTAL, :].astype(jnp.float32)
    return rows[0:1] + rows[1:2]


def read_state(ref, h):
    return ref[h, 0:DIM, :].astype(jnp.float32)


def write(ref, h, state, total):
    ref[h, 0:DIM, :] = state.astype(jnp.bfloat16)
    ref[h, DIM : DIM + TOTAL, :] = total_rows(total)


def local_state_kernel(k_ref, v_ref, g_ref, mine_ref, theirs_ref):
    core = lax.axis_index("ctx_2")
    cum = running_sum(g_ref[...])
    cum_t = columns(cum)
    for h in range(HEADS):
        cols = slice(h * DIM, (h + 1) * DIM)
        last = cum[h : h + 1, CH - 1 : CH]
        scale = jnp.exp(last - cum_t[:, h : h + 1])
        ks = (k_ref[:, cols].astype(jnp.float32) * scale).astype(jnp.bfloat16)
        local = dot(ks, v_ref[:, cols], TN)

        @pl.when(core == h // HALF)
        def _():
            write(mine_ref, h % HALF, local, last)

        @pl.when(core != h // HALF)
        def _():
            write(theirs_ref, h % HALF, local, last)


def in_order(core, mine_ref, other_ref, h):
    a, b = read_state(mine_ref, h), read_state(other_ref, h)
    ta, tb = read_total(mine_ref, h), read_total(other_ref, h)
    own = core == 0
    return jnp.where(own, a, b), jnp.where(own, ta, tb), jnp.where(own, b, a), jnp.where(own, tb, ta)


def chip_state_kernel(mine_ref, other_ref, chip_ref):
    core = lax.axis_index("ctx_2")
    for h in range(HALF):
        s0, t0, s1, t1 = in_order(core, mine_ref, other_ref, h)
        write(chip_ref, h, jnp.exp(t1) * s0 + s1, t0 + t1)


def row_state_kernel(own_ref, a_ref, b_ref, c_ref, row_ref, before_ref, all_ref):
    my = lax.axis_index("ctx_1")
    for d, ref in enumerate((own_ref, a_ref, b_ref, c_ref)):
        all_ref[(my + NY - d) % NY] = ref[...]
    for h in range(HALF):
        state = jnp.zeros((DIM, DIM), jnp.float32)
        total = jnp.zeros((1, DIM), jnp.float32)
        before, before_total = state, total
        for y in range(NY):
            here = my == y
            before = jnp.where(here, state, before)
            before_total = jnp.where(here, total, before_total)
            t = read_total(all_ref.at[y], h)
            state = jnp.exp(t) * state + read_state(all_ref.at[y], h)
            total = total + t
        write(row_ref, h, state, total)
        before_ref[h, 0:DIM, :] = before
        before_ref[h, DIM : DIM + 8, :] = jnp.broadcast_to(before_total, (8, DIM))


def entering_kernel(a_ref, b_ref, c_ref, before_ref, mine_ref, other_ref, keep_ref, send_ref):
    mx, core = lax.axis_index("ctx_0"), lax.axis_index("ctx_2")
    for h in range(HALF):
        state = jnp.zeros((DIM, DIM), jnp.float32)
        for d, ref in ((3, c_ref), (2, b_ref), (1, a_ref)):
            new = jnp.exp(read_total(ref, h)) * state + read_state(ref, h)
            state = jnp.where(mx >= d, new, state)
        state = jnp.exp(before_ref[h, DIM : DIM + 1, :]) * state + before_ref[h, 0:DIM, :]
        s0, t0, _, _ = in_order(core, mine_ref, other_ref, h)
        later = jnp.exp(t0) * state + s0
        keep_ref[h] = jnp.where(core == 0, state, later).astype(jnp.bfloat16)
        send_ref[h] = jnp.where(core == 0, later, state).astype(jnp.bfloat16)


def lightning_kernel(q_ref, k_ref, v_ref, g_ref, gain_ref, keep_ref, got_ref, out_ref):
    core = lax.axis_index("ctx_2")
    cum = running_sum(g_ref[...])
    cum_t = columns(cum)
    causal = lax.broadcasted_iota(jnp.int32, (CH, CH), 0) >= lax.broadcasted_iota(
        jnp.int32, (CH, CH), 1
    )
    for h in range(HEADS):
        cols = slice(h * DIM, (h + 1) * DIM)
        q, k, v = q_ref[:, cols], k_ref[:, cols], v_ref[:, cols]
        col = cum_t[:, h : h + 1]
        diff = jnp.minimum(col - cum[h : h + 1, :], 0.0)
        weight = jnp.where(causal, jnp.exp(diff), 0.0)
        probs = (dot(q, k, NT) * weight).astype(jnp.bfloat16)
        state = jnp.where(core == h // HALF, keep_ref[h % HALF], got_ref[h % HALF])
        mix = dot(probs, v, NN) + jnp.exp(col) * dot(q, state, NN)
        norm = lax.rsqrt(jnp.mean(mix * mix, axis=1, keepdims=True) + 1e-05)
        out_ref[:, cols] = (mix * norm * gain_ref[:, cols]).astype(jnp.bfloat16)


ROWS = HEADS * 64
KEYS = NY * NC * CH
SCALE = math.log2(math.e) / math.sqrt(DIM)


def softmax_kernel(*refs):
    q_ref = refs[0]
    pieces = refs[1:11]
    out_ref, kv_ref, qq_ref, s_ref, p_ref, pm_ref, al_ref, m_ref, acc_ref, sems = refs[11:]
    mx, my, mc = (lax.axis_index(a) for a in CTX)
    yc = my * NC + mc

    def fetch(ref, at, chunk):
        return pltpu.make_async_copy(
            ref.at[pl.ds(at * CH, CH), :],
            kv_ref.at[pl.ds(pl.multiple_of(chunk * CH, CH), CH), :],
            sems.at[chunk],
        )

    for late in (False, True):
        for other in range(2):
            row, plus, minus, far_a, far_b = pieces[5 * other : 5 * other + 5]
            core = mc if other == 0 else 1 - mc
            for ds, source in ((0, row), (1, plus), (3, minus), (2, None)):
                for slot, df in enumerate((0, 1, 3, 2)):
                    ref, at = source, slot
                    if source is None:
                        ref, at = (far_a, slot) if slot < 2 else (far_b, slot - 2)
                    x = (mx + NX - jnp.where(core == 0, df, ds)) % NX
                    y = (my + NY - jnp.where(core == 0, ds, df)) % NY

                    @pl.when((x >= 2) == late)
                    def _():
                        fetch(ref, at, (x * NY + y) * NC + core).start()

    def arrived(x):
        for i in range(NY * NC):
            fetch(pieces[0], 0, x * NY * NC + i).wait()

    for x in range(NX):
        for g in range(HEADS):
            rows = slice(x * ROWS + g * 64, x * ROWS + (g + 1) * 64)
            qq_ref[rows, :] = q_ref[x * 64 : (x + 1) * 64, g * DIM : (g + 1) * DIM]
    acc_ref[...] = jnp.zeros_like(acc_ref)

    tiles = NX * (NX + 1) // 2

    def tile(t):
        t = jnp.int32(t)
        x = sum((t >= n).astype(jnp.int32) for n in (1, 3, 6))
        u = t - x * (x + 1) // 2
        return x, u, jnp.where(u == 0, x, u - 1) * KEYS, t % 2

    def scores(t):
        x, _, start, slot = tile(t)
        r = lax.broadcasted_iota(jnp.int32, (ROWS, 1), 0) % 64
        pos = (x * 8 + yc) * CH + (r // 8) * 32 + mx * 8 + r % 8 - start
        qq = qq_ref[pl.ds(pl.multiple_of(x * ROWS, ROWS), ROWS), :]
        for k in range(KEYS // 256):
            keys = kv_ref[pl.ds(pl.multiple_of(start + k * 256, 256), 256), 0:DIM]
            s = dot(qq, keys, NT) * SCALE
            lane = lax.broadcasted_iota(jnp.int32, s.shape, 1)
            s = jnp.where(lane <= pos - k * 256, s, -1e30)
            s_ref[slot, :, k * 256 : (k + 1) * 256] = s
            peak = jnp.maximum(s[:, :DIM], s[:, DIM:])
            if k > 0:
                peak = jnp.maximum(peak, pm_ref[slot])
            if k == KEYS // 256 - 1:
                peak = jnp.broadcast_to(jnp.max(peak, axis=1, keepdims=True), (ROWS, DIM))
            pm_ref[slot] = peak

    def weights(t):
        _, u, _, slot = tile(t)
        for i in range(ROWS // 64):
            rows = slice(i * 64, (i + 1) * 64)
            old = jnp.where(u == 0, -1e30, m_ref[rows, :])
            new = jnp.maximum(old, pm_ref[slot, rows, :])
            al_ref[slot, rows, :] = jnp.exp2(old - new)
            m_ref[rows, :] = new
            for k in range(KEYS // DIM):
                cols = slice(k * DIM, (k + 1) * DIM)
                p_ref[slot, rows, cols] = jnp.exp2(s_ref[slot, rows, cols] - new).astype(
                    jnp.bfloat16
                )

    def mix(t):
        _, _, start, slot = tile(t)
        values = kv_ref[pl.ds(pl.multiple_of(start, KEYS), KEYS), DIM : 2 * DIM]
        values = jnp.concatenate([values, jnp.ones_like(values)], axis=1)
        alpha = al_ref[slot]
        alpha = jnp.concatenate([alpha, alpha], axis=1)
        acc_ref[...] = acc_ref[...] * alpha + dot(p_ref[slot], values, NN)

    def finish(t):
        x, u, _, _ = tile(t)

        @pl.when(u == x)
        def _():
            for g in range(HEADS):
                rows = slice(g * 64, (g + 1) * 64)
                o = acc_ref[rows, 0:DIM] / acc_ref[rows, DIM : 2 * DIM]
                out_ref[pl.ds(pl.multiple_of(x * 64, 64), 64), g * DIM : (g + 1) * DIM] = o.astype(
                    jnp.bfloat16
                )

    arrived(0)
    scores(0)
    arrived(1)
    weights(0)
    scores(1)

    @pl.loop(0, tiles - 2)
    def _(t):
        for x, first in ((2, 3), (3, 6)):
            pl.when(t + 2 == first)(functools.partial(arrived, x))
        mix(t)
        scores(t + 2)
        weights(t + 1)
        finish(t)

    mix(tiles - 2)
    weights(tiles - 1)
    mix(tiles - 1)
    finish(tiles - 1)


def vmem(n):
    return [pl.BlockSpec(memory_space=pltpu.VMEM)] * n


def call(kernel, outs, n, flops, **kw):
    return pl.pallas_call(
        kernel,
        out_shape=[jax.ShapeDtypeStruct(*o) for o in outs],
        in_specs=kw.pop("in_specs", vmem(n)),
        out_specs=vmem(len(outs)),
        compiler_params=pltpu.CompilerParams(vmem_limit_bytes=kw.pop("limit", 32 << 20)),
        cost_estimate=pl.CostEstimate(flops=flops, bytes_accessed=2 << 20, transcendentals=0),
        **kw,
    )


def ctx_index(x, y, c):
    return (x % NX * NY + y % NY) * NC + c


def ring(first, sign):
    pairs = []
    for x in range(NX):
        for y in range(NY):
            for c in range(NC):
                along_x = (c == 0) == first
                to = (x + sign, y) if along_x else (x, y + sign)
                pairs.append((ctx_index(x, y, c), ctx_index(*to, c)))
    return pairs


def permute(value, pairs, axes=CTX):
    return lax.ppermute(value, axes, pairs)


def exchange(value, axes):
    return lax.all_to_all(value, axes, 0, 0, tiled=True)


def gather_kv(own):
    r1 = permute(own, ring(True, 1))
    r2 = permute(own, ring(True, -1))
    r3 = permute(own, ring(True, 2))
    row = jnp.concatenate([own, r1, r2, r3], axis=0)
    s1 = permute(row, ring(False, 1))
    s2 = permute(row, ring(False, -1))
    t1 = permute(s1[: 2 * CH], ring(False, 1))
    t2 = permute(s2[2 * CH :], ring(False, -1))
    mine = [row, s1, s2, t1, t2]
    swap = [(0, 1), (1, 0)]
    return mine + [permute(p, swap, "ctx_2") for p in mine]


def both(lin_q, lin_k, lin_v, log_decay, lin_gain, soft_q, soft_kv):
    kv = soft_kv.reshape(32, NZ, 2 * DIM).swapaxes(0, 1)
    kv = exchange(kv, "head").reshape(CH, 2 * DIM)
    q = soft_q.reshape(NX, 8, NZ, HEADS * DIM).swapaxes(1, 2).reshape(NX * NZ, 8, HEADS * DIM)
    q = exchange(q, ("ctx_0", "head")).reshape(CH, HEADS * DIM)
    pieces = gather_kv(kv)

    swap = [(0, 1), (1, 0)]
    msg = (HALF, DIM + TOTAL, DIM)
    msg16 = (msg, jnp.bfloat16)
    entering = ((HALF, DIM, DIM), jnp.bfloat16)
    mine, theirs = call(local_state_kernel, [msg16] * 2, 3, 1 << 28)(lin_k, lin_v, log_decay)
    other = permute(theirs, swap, "ctx_2")
    (chip,) = call(chip_state_kernel, [msg16], 2, 1 << 20)(mine, other)
    around = [permute(chip, [(y, (y + d) % NY) for y in range(NY)], "ctx_1") for d in (1, 2, 3)]
    row_state, before = call(
        row_state_kernel,
        [msg16, (msg, jnp.float32)],
        4,
        1 << 20,
        scratch_shapes=[pltpu.VMEM((NY, *msg), jnp.bfloat16)],
    )(chip, *around)
    earlier = [permute(row_state, [(x, x + d) for x in range(NX - d)], "ctx_0") for d in (1, 2, 3)]
    keep, send = call(entering_kernel, [entering] * 2, 6, 1 << 20)(*earlier, before, mine, other)
    got = permute(send, swap, "ctx_2")

    block = ((CH, HEADS * DIM), jnp.bfloat16)
    (soft,) = call(
        softmax_kernel,
        [block],
        11,
        1 << 34,
        in_specs=vmem(1) + [pl.BlockSpec(memory_space=pl.ANY)] * 10,
        limit=22 << 20,
        scratch_shapes=[
            pltpu.VMEM((NX * NY * NC * CH, 2 * DIM), jnp.bfloat16),
            pltpu.VMEM((NX * ROWS, DIM), jnp.bfloat16),
            pltpu.VMEM((2, ROWS, KEYS), jnp.float32),
            pltpu.VMEM((2, ROWS, KEYS), jnp.bfloat16),
            pltpu.VMEM((2, ROWS, DIM), jnp.float32),
            pltpu.VMEM((2, ROWS, DIM), jnp.float32),
            pltpu.VMEM((ROWS, DIM), jnp.float32),
            pltpu.VMEM((ROWS, 2 * DIM), jnp.float32),
            pltpu.SemaphoreType.DMA((32,)),
        ],
    )(q, *pieces)
    soft = exchange(soft.reshape(NX * NZ, 8, HEADS * DIM), ("ctx_0", "head"))
    soft_out = soft.reshape(NX, NZ, 8, HEADS * DIM).swapaxes(1, 2).reshape(32, NZ * HEADS * DIM)

    (lin_out,) = call(lightning_kernel, [block], 7, 1 << 29)(
        lin_q, lin_k, lin_v, log_decay, lin_gain.reshape(1, -1), keep, got
    )
    return (lin_out, soft_out)


def solution(mesh):
    finer = Mesh(
        mesh.devices.reshape(NX, NY, NC, NZ), ("ctx_0", "ctx_1", "ctx_2", "head")
    )
    placed = (
        P(CTX, "head"),
        P(CTX, "head"),
        P(CTX, "head"),
        P("head", CTX),
        P("head"),
        P(CTX_HEAD, None),
        P(CTX_HEAD, None),
    )
    return jax.shard_map(
        both,
        mesh=finer,
        in_specs=placed,
        out_specs=(P(CTX, "head"), P(CTX_HEAD, None)),
        check_vma=False,
    )
```

```python
import math

import jax
import jax.numpy as jnp
from jax import lax
from jax.experimental import pallas as pl
from jax.experimental.pallas import tpu as pltpu
from jax.sharding import Mesh
from jax.sharding import PartitionSpec as P

CTX = ("ctx_0", "ctx_1", "ctx_2")
CTX_HEAD = ("ctx_0", "ctx_1", "ctx_2", "head")
NX, NY, NC, NZ = 4, 4, 2, 8
CH = 256
DIM = 128
HEADS = 8
HALF = HEADS // 2
TOTAL = 16

NT = (((1,), (1,)), ((), ()))
NN = (((1,), (0,)), ((), ()))
TN = (((0,), (0,)), ((), ()))


def dot(a, b, dims):
    return lax.dot_general(a, b, dims, preferred_element_type=jnp.float32)


def running_sum(g):
    lane = lax.broadcasted_iota(jnp.int32, g.shape, 1)
    step = 1
    while step < g.shape[1]:
        g = g + jnp.where(lane >= step, pltpu.roll(g, step, 1), 0.0)
        step *= 2
    return g


def columns(cum):
    wide = jnp.concatenate([cum, jnp.zeros((DIM - cum.shape[0], cum.shape[1]), cum.dtype)], 0)
    return wide.T


def total_rows(total):
    row = lax.broadcasted_iota(jnp.int32, (TOTAL, DIM), 0)
    total = jnp.broadcast_to(total, (TOTAL, DIM))
    high = total.astype(jnp.bfloat16).astype(jnp.float32)
    return jnp.where(row == 0, high, jnp.where(row == 1, total - high, 0.0)).astype(jnp.bfloat16)


def read_total(ref, h):
    rows = ref[h, DIM : DIM + TOTAL, :].astype(jnp.float32)
    return rows[0:1] + rows[1:2]


def read_state(ref, h):
    return ref[h, 0:DIM, :].astype(jnp.float32)


def write(ref, h, state, total):
    ref[h, 0:DIM, :] = state.astype(jnp.bfloat16)
    ref[h, DIM : DIM + TOTAL, :] = total_rows(total)


def local_state_kernel(k_ref, v_ref, g_ref, mine_ref, theirs_ref):
    first = lax.axis_index("ctx_2") == 0
    cum = running_sum(g_ref[...])
    cum_t = columns(cum)

    def local(h):
        cols = slice(h * DIM, (h + 1) * DIM)
        last = cum[h : h + 1, CH - 1 : CH]
        scale = jnp.exp(last - cum_t[:, h : h + 1])
        ks = (k_ref[:, cols].astype(jnp.float32) * scale).astype(jnp.bfloat16)
        return dot(ks, v_ref[:, cols], TN), last

    for h in range(HALF):
        low, low_total = local(h)
        high, high_total = local(HALF + h)
        write(
            mine_ref, h, jnp.where(first, low, high), jnp.where(first, low_total, high_total)
        )
        write(
            theirs_ref, h, jnp.where(first, high, low), jnp.where(first, high_total, low_total)
        )


def in_order(core, mine_ref, other_ref, h):
    a, b = read_state(mine_ref, h), read_state(other_ref, h)
    ta, tb = read_total(mine_ref, h), read_total(other_ref, h)
    own = core == 0
    return jnp.where(own, a, b), jnp.where(own, ta, tb), jnp.where(own, b, a), jnp.where(own, tb, ta)


def chip_state_kernel(mine_ref, other_ref, chip_ref):
    core = lax.axis_index("ctx_2")
    for h in range(HALF):
        s0, t0, s1, t1 = in_order(core, mine_ref, other_ref, h)
        write(chip_ref, h, jnp.exp(t1) * s0 + s1, t0 + t1)


def row_state_kernel(own_ref, a_ref, b_ref, c_ref, row_ref, before_ref, all_ref):
    my = lax.axis_index("ctx_1")
    for d, ref in enumerate((own_ref, a_ref, b_ref, c_ref)):
        all_ref[(my + NY - d) % NY] = ref[...]
    for h in range(HALF):
        state = jnp.zeros((DIM, DIM), jnp.float32)
        total = jnp.zeros((1, DIM), jnp.float32)
        before, before_total = state, total
        for y in range(NY):
            here = my == y
            before = jnp.where(here, state, before)
            before_total = jnp.where(here, total, before_total)
            t = read_total(all_ref.at[y], h)
            state = jnp.exp(t) * state + read_state(all_ref.at[y], h)
            total = total + t
        write(row_ref, h, state, total)
        before_ref[h, 0:DIM, :] = before
        before_ref[h, DIM : DIM + 8, :] = jnp.broadcast_to(before_total, (8, DIM))


def entering_kernel(a_ref, b_ref, c_ref, before_ref, mine_ref, other_ref, keep_ref, send_ref):
    mx, core = lax.axis_index("ctx_0"), lax.axis_index("ctx_2")
    for h in range(HALF):
        state = jnp.zeros((DIM, DIM), jnp.float32)
        for d, ref in ((3, c_ref), (2, b_ref), (1, a_ref)):
            new = jnp.exp(read_total(ref, h)) * state + read_state(ref, h)
            state = jnp.where(mx >= d, new, state)
        state = jnp.exp(before_ref[h, DIM : DIM + 1, :]) * state + before_ref[h, 0:DIM, :]
        s0, t0, _, _ = in_order(core, mine_ref, other_ref, h)
        later = jnp.exp(t0) * state + s0
        keep_ref[h] = jnp.where(core == 0, state, later).astype(jnp.bfloat16)
        send_ref[h] = jnp.where(core == 0, later, state).astype(jnp.bfloat16)


def lightning_kernel(q_ref, k_ref, v_ref, g_ref, gain_ref, keep_ref, got_ref, out_ref):
    core = lax.axis_index("ctx_2")
    cum = running_sum(g_ref[...])
    cum_t = columns(cum)
    causal = lax.broadcasted_iota(jnp.int32, (CH, CH), 0) >= lax.broadcasted_iota(
        jnp.int32, (CH, CH), 1
    )
    for h in range(HEADS):
        cols = slice(h * DIM, (h + 1) * DIM)
        q, k, v = q_ref[:, cols], k_ref[:, cols], v_ref[:, cols]
        col = cum_t[:, h : h + 1]
        diff = jnp.minimum(col - cum[h : h + 1, :], 0.0)
        weight = jnp.where(causal, jnp.exp(diff), 0.0)
        probs = (dot(q, k, NT) * weight).astype(jnp.bfloat16)
        state = jnp.where(core == h // HALF, keep_ref[h % HALF], got_ref[h % HALF])
        mix = dot(probs, v, NN) + jnp.exp(col) * dot(q, state, NN)
        norm = lax.rsqrt(jnp.mean(mix * mix, axis=1, keepdims=True) + 1e-05)
        out_ref[:, cols] = (mix * norm * gain_ref[:, cols]).astype(jnp.bfloat16)


ROWS = HEADS * 64
KEYS = NY * NC * CH
SCALE = math.log2(math.e) / math.sqrt(DIM)


def softmax_kernel(*refs):
    q_ref = refs[0]
    pieces = refs[1:11]
    out_ref, kv_ref, qq_ref, s_ref, p_ref, pm_ref, al_ref, m_ref, acc_ref, sems = refs[11:]
    mx, my, mc = (lax.axis_index(a) for a in CTX)
    yc = my * NC + mc

    copies = []
    for n, ref in enumerate(pieces):
        other, part = divmod(n, 5)
        rows = pl.ds((other * 16 + (0, 4, 8, 12, 14)[part]) * CH, ref.shape[0])
        copies.append(pltpu.make_async_copy(ref, kv_ref.at[rows, :], sems.at[n]))
        copies[-1].start()

    def chunk(kx, k):
        other, i = divmod(k, 4)
        core = mc if other == 0 else 1 - mc
        d = (mx + NX - kx) % NX
        d = jnp.where(d < 2, d, 5 - d)
        slot = other * 16 + jnp.where(core == 0, i * 4 + d, d * 4 + i)
        y = (my + NY - (0, 1, 3, 2)[i]) % NY
        return pl.ds(pl.multiple_of(slot * CH, CH), CH), (y * NC + core) * CH

    for x in range(NX):
        for g in range(HEADS):
            rows = slice(x * ROWS + g * 64, x * ROWS + (g + 1) * 64)
            qq_ref[rows, :] = q_ref[x * 64 : (x + 1) * 64, g * DIM : (g + 1) * DIM]
    acc_ref[...] = jnp.zeros_like(acc_ref)
    for copy in copies:
        copy.wait()

    tiles = NX * (NX + 1) // 2

    def tile(t):
        t = jnp.int32(t)
        x = sum((t >= n).astype(jnp.int32) for n in (1, 3, 6))
        u = t - x * (x + 1) // 2
        return x, u, jnp.where(u == 0, x, u - 1), t % 2

    def scores(t):
        x, _, kx, slot = tile(t)
        r = lax.broadcasted_iota(jnp.int32, (ROWS, 1), 0) % 64
        pos = ((x - kx) * 8 + yc) * CH + (r // 8) * 32 + mx * 8 + r % 8
        qq = qq_ref[pl.ds(pl.multiple_of(x * ROWS, ROWS), ROWS), :]
        for k in range(KEYS // CH):
            rows, at = chunk(kx, k)
            s = dot(qq, kv_ref[rows, 0:DIM], NT) * SCALE
            lane = lax.broadcasted_iota(jnp.int32, s.shape, 1)
            s = jnp.where(lane <= pos - at, s, -1e30)
            s_ref[slot, :, k * CH : (k + 1) * CH] = s
            peak = jnp.maximum(s[:, :DIM], s[:, DIM:])
            if k > 0:
                peak = jnp.maximum(peak, pm_ref[slot])
            if k == KEYS // CH - 1:
                peak = jnp.broadcast_to(jnp.max(peak, axis=1, keepdims=True), (ROWS, DIM))
            pm_ref[slot] = peak

    def weights(t):
        _, u, _, slot = tile(t)
        for i in range(ROWS // 64):
            rows = slice(i * 64, (i + 1) * 64)
            old = jnp.where(u == 0, -1e30, m_ref[rows, :])
            new = jnp.maximum(old, pm_ref[slot, rows, :])
            al_ref[slot, rows, :] = jnp.exp2(old - new)
            m_ref[rows, :] = new
            for k in range(KEYS // DIM):
                cols = slice(k * DIM, (k + 1) * DIM)
                p_ref[slot, rows, cols] = jnp.exp2(s_ref[slot, rows, cols] - new).astype(
                    jnp.bfloat16
                )

    def mix(t):
        _, _, kx, slot = tile(t)
        values = [kv_ref[chunk(kx, k)[0], DIM : 2 * DIM] for k in range(KEYS // CH)]
        values = jnp.concatenate(values, axis=0)
        values = jnp.concatenate([values, jnp.ones_like(values)], axis=1)
        alpha = al_ref[slot]
        alpha = jnp.concatenate([alpha, alpha], axis=1)
        acc_ref[...] = acc_ref[...] * alpha + dot(p_ref[slot], values, NN)

    def finish(t):
        x, u, _, _ = tile(t)

        @pl.when(u == x)
        def _():
            for g in range(HEADS):
                rows = slice(g * 64, (g + 1) * 64)
                o = acc_ref[rows, 0:DIM] / acc_ref[rows, DIM : 2 * DIM]
                out_ref[pl.ds(pl.multiple_of(x * 64, 64), 64), g * DIM : (g + 1) * DIM] = o.astype(
                    jnp.bfloat16
                )

    scores(0)
    weights(0)
    scores(1)

    @pl.loop(0, tiles - 2)
    def _(t):
        mix(t)
        scores(t + 2)
        weights(t + 1)
        finish(t)

    mix(tiles - 2)
    weights(tiles - 1)
    mix(tiles - 1)
    finish(tiles - 1)


def vmem(n):
    return [pl.BlockSpec(memory_space=pltpu.VMEM)] * n


def call(kernel, outs, n, flops, **kw):
    return pl.pallas_call(
        kernel,
        out_shape=[jax.ShapeDtypeStruct(*o) for o in outs],
        in_specs=kw.pop("in_specs", vmem(n)),
        out_specs=vmem(len(outs)),
        compiler_params=pltpu.CompilerParams(vmem_limit_bytes=kw.pop("limit", 32 << 20)),
        cost_estimate=pl.CostEstimate(flops=flops, bytes_accessed=2 << 20, transcendentals=0),
        **kw,
    )


def ctx_index(x, y, c):
    return (x % NX * NY + y % NY) * NC + c


def ring(first, sign):
    pairs = []
    for x in range(NX):
        for y in range(NY):
            for c in range(NC):
                along_x = (c == 0) == first
                to = (x + sign, y) if along_x else (x, y + sign)
                pairs.append((ctx_index(x, y, c), ctx_index(*to, c)))
    return pairs


def permute(value, pairs, axes=CTX):
    return lax.ppermute(value, axes, pairs)


def exchange(value, axes):
    return lax.all_to_all(value, axes, 0, 0, tiled=True)


def gather_kv(own):
    r1 = permute(own, ring(True, 1))
    r2 = permute(own, ring(True, -1))
    r3 = permute(own, ring(True, 2))
    row = jnp.concatenate([own, r1, r2, r3], axis=0)
    s1 = permute(row, ring(False, 1))
    s2 = permute(row, ring(False, -1))
    t1 = permute(s1[: 2 * CH], ring(False, 1))
    t2 = permute(s2[2 * CH :], ring(False, -1))
    mine = [row, s1, s2, t1, t2]
    swap = [(0, 1), (1, 0)]
    return mine + [permute(p, swap, "ctx_2") for p in mine]


def both(lin_q, lin_k, lin_v, log_decay, lin_gain, soft_q, soft_kv):
    kv = soft_kv.reshape(32, NZ, 2 * DIM).swapaxes(0, 1)
    kv = exchange(kv, "head").reshape(CH, 2 * DIM)
    q = soft_q.reshape(NX, 8, NZ, HEADS * DIM).swapaxes(1, 2).reshape(NX * NZ, 8, HEADS * DIM)
    q = exchange(q, ("ctx_0", "head")).reshape(CH, HEADS * DIM)
    pieces = gather_kv(kv)

    swap = [(0, 1), (1, 0)]
    msg = (HALF, DIM + TOTAL, DIM)
    msg16 = (msg, jnp.bfloat16)
    entering = ((HALF, DIM, DIM), jnp.bfloat16)
    mine, theirs = call(local_state_kernel, [msg16] * 2, 3, 1 << 28)(lin_k, lin_v, log_decay)
    other = permute(theirs, swap, "ctx_2")
    (chip,) = call(chip_state_kernel, [msg16], 2, 1 << 20)(mine, other)
    around = [permute(chip, [(y, (y + d) % NY) for y in range(NY)], "ctx_1") for d in (1, 2, 3)]
    row_state, before = call(
        row_state_kernel,
        [msg16, (msg, jnp.float32)],
        4,
        1 << 20,
        scratch_shapes=[pltpu.VMEM((NY, *msg), jnp.bfloat16)],
    )(chip, *around)
    earlier = [permute(row_state, [(x, x + d) for x in range(NX - d)], "ctx_0") for d in (1, 2, 3)]
    keep, send = call(entering_kernel, [entering] * 2, 6, 1 << 20)(*earlier, before, mine, other)
    got = permute(send, swap, "ctx_2")

    block = ((CH, HEADS * DIM), jnp.bfloat16)
    (soft,) = call(
        softmax_kernel,
        [block],
        11,
        1 << 34,
        in_specs=vmem(1) + [pl.BlockSpec(memory_space=pl.ANY)] * 10,
        limit=28 << 20,
        scratch_shapes=[
            pltpu.VMEM((NX * NY * NC * CH, 2 * DIM), jnp.bfloat16),
            pltpu.VMEM((NX * ROWS, DIM), jnp.bfloat16),
            pltpu.VMEM((2, ROWS, KEYS), jnp.float32),
            pltpu.VMEM((2, ROWS, KEYS), jnp.bfloat16),
            pltpu.VMEM((2, ROWS, DIM), jnp.float32),
            pltpu.VMEM((2, ROWS, DIM), jnp.float32),
            pltpu.VMEM((ROWS, DIM), jnp.float32),
            pltpu.VMEM((ROWS, 2 * DIM), jnp.float32),
            pltpu.SemaphoreType.DMA((10,)),
        ],
    )(q, *pieces)
    soft = exchange(soft.reshape(NX * NZ, 8, HEADS * DIM), ("ctx_0", "head"))
    soft_out = soft.reshape(NX, NZ, 8, HEADS * DIM).swapaxes(1, 2).reshape(32, NZ * HEADS * DIM)

    (lin_out,) = call(lightning_kernel, [block], 7, 1 << 29)(
        lin_q, lin_k, lin_v, log_decay, lin_gain.reshape(1, -1), keep, got
    )
    return (lin_out, soft_out)


def solution(mesh):
    finer = Mesh(
        mesh.devices.reshape(NX, NY, NC, NZ), ("ctx_0", "ctx_1", "ctx_2", "head")
    )
    placed = (
        P(CTX, "head"),
        P(CTX, "head"),
        P(CTX, "head"),
        P("head", CTX),
        P("head"),
        P(CTX_HEAD, None),
        P(CTX_HEAD, None),
    )
    return jax.shard_map(
        both,
        mesh=finer,
        in_specs=placed,
        out_specs=(P(CTX, "head"), P(CTX_HEAD, None)),
        check_vma=False,
    )
```

```python
import math

import jax
import jax.numpy as jnp
from jax import lax
from jax.experimental import pallas as pl
from jax.experimental.pallas import tpu as pltpu
from jax.sharding import Mesh
from jax.sharding import PartitionSpec as P

CTX = ("ctx_0", "ctx_1", "ctx_2")
CTX_HEAD = ("ctx_0", "ctx_1", "ctx_2", "head")
NX, NY, NC, NZ = 4, 4, 2, 8
CH = 256
DIM = 128
HEADS = 8
HALF = HEADS // 2
TOTAL = 16

NT = (((1,), (1,)), ((), ()))
NN = (((1,), (0,)), ((), ()))
TN = (((0,), (0,)), ((), ()))


def dot(a, b, dims):
    return lax.dot_general(a, b, dims, preferred_element_type=jnp.float32)


def running_sum(g):
    lane = lax.broadcasted_iota(jnp.int32, g.shape, 1)
    step = 1
    while step < g.shape[1]:
        g = g + jnp.where(lane >= step, pltpu.roll(g, step, 1), 0.0)
        step *= 2
    return g


def columns(cum):
    wide = jnp.concatenate([cum, jnp.zeros((DIM - cum.shape[0], cum.shape[1]), cum.dtype)], 0)
    return wide.T


def total_rows(total):
    row = lax.broadcasted_iota(jnp.int32, (TOTAL, DIM), 0)
    total = jnp.broadcast_to(total, (TOTAL, DIM))
    high = total.astype(jnp.bfloat16).astype(jnp.float32)
    return jnp.where(row == 0, high, jnp.where(row == 1, total - high, 0.0)).astype(jnp.bfloat16)


def read_total(ref):
    rows = ref[DIM : DIM + TOTAL, :].astype(jnp.float32)
    return rows[0:1] + rows[1:2]


def read_state(ref):
    return ref[0:DIM, :].astype(jnp.float32)


def write(ref, state, total):
    ref[0:DIM, :] = state.astype(jnp.bfloat16)
    ref[DIM : DIM + TOTAL, :] = total_rows(total)


def local_state_kernel(k_ref, v_ref, g_ref, mine_ref, theirs_ref):
    first = lax.axis_index("ctx_2") == 0
    cum = running_sum(g_ref[...])
    cum_t = columns(cum)

    def local(h):
        cols = slice(h * DIM, (h + 1) * DIM)
        last = cum[h : h + 1, CH - 1 : CH]
        scale = jnp.exp(last - cum_t[:, h : h + 1])
        ks = (k_ref[:, cols].astype(jnp.float32) * scale).astype(jnp.bfloat16)
        return dot(ks, v_ref[:, cols], TN), last

    for h in range(HALF):
        low, low_total = local(h)
        high, high_total = local(HALF + h)
        write(
            mine_ref.at[h], jnp.where(first, low, high), jnp.where(first, low_total, high_total)
        )
        write(
            theirs_ref.at[h], jnp.where(first, high, low), jnp.where(first, high_total, low_total)
        )


def in_order(first, mine_ref, other_ref):
    a, b = read_state(mine_ref), read_state(other_ref)
    ta, tb = read_total(mine_ref), read_total(other_ref)
    return (
        jnp.where(first, a, b),
        jnp.where(first, ta, tb),
        jnp.where(first, b, a),
        jnp.where(first, tb, ta),
    )


def chip_state_kernel(mine_ref, other_ref, *chip_refs):
    my, first = lax.axis_index("ctx_1"), lax.axis_index("ctx_2") == 0
    for d, chip_ref in enumerate(chip_refs):
        h = (my + d) % NY
        s0, t0, s1, t1 = in_order(first, mine_ref.at[h], other_ref.at[h])
        write(chip_ref, jnp.exp(t1) * s0 + s1, t0 + t1)


def row_state_kernel(own_ref, a_ref, b_ref, c_ref, row_ref, before_ref, all_ref):
    my = lax.axis_index("ctx_1")
    for d, ref in enumerate((own_ref, a_ref, b_ref, c_ref)):
        all_ref[(my + NY - d) % NY] = ref[...]
    state = jnp.zeros((DIM, DIM), jnp.float32)
    total = jnp.zeros((1, DIM), jnp.float32)
    for y in range(NY):
        before_ref[y, 0:DIM, :] = state
        before_ref[y, DIM : DIM + 8, :] = jnp.broadcast_to(total, (8, DIM))
        t = read_total(all_ref.at[y])
        state = jnp.exp(t) * state + read_state(all_ref.at[y])
        total = total + t
    write(row_ref, state, total)


def enter_row_kernel(a_ref, b_ref, c_ref, before_ref, *out_refs):
    mx, my = lax.axis_index("ctx_0"), lax.axis_index("ctx_1")
    state = jnp.zeros((DIM, DIM), jnp.float32)
    for d, ref in ((3, c_ref), (2, b_ref), (1, a_ref)):
        new = jnp.exp(read_total(ref)) * state + read_state(ref)
        state = jnp.where(mx >= d, new, state)
    for d, out_ref in enumerate(out_refs):
        y = (my + d) % NY
        before = before_ref[y]
        out = jnp.exp(before[DIM : DIM + 1]) * state + before[0:DIM]
        out_ref[...] = out.astype(jnp.bfloat16)


def enter_chunk_kernel(e0_ref, e1_ref, e2_ref, e3_ref, mine_ref, other_ref, keep_ref, send_ref):
    my, first = lax.axis_index("ctx_1"), lax.axis_index("ctx_2") == 0
    for d, ref in enumerate((e0_ref, e1_ref, e2_ref, e3_ref)):
        h = (my + NY - d) % NY
        state = ref[...].astype(jnp.float32)
        s0, t0, _, _ = in_order(first, mine_ref.at[h], other_ref.at[h])
        later = jnp.exp(t0) * state + s0
        keep_ref[h] = jnp.where(first, state, later).astype(jnp.bfloat16)
        send_ref[h] = jnp.where(first, later, state).astype(jnp.bfloat16)


def lightning_kernel(q_ref, k_ref, v_ref, g_ref, gain_ref, keep_ref, got_ref, out_ref):
    core = lax.axis_index("ctx_2")
    cum = running_sum(g_ref[...])
    cum_t = columns(cum)
    causal = lax.broadcasted_iota(jnp.int32, (CH, CH), 0) >= lax.broadcasted_iota(
        jnp.int32, (CH, CH), 1
    )
    for h in range(HEADS):
        cols = slice(h * DIM, (h + 1) * DIM)
        q, k, v = q_ref[:, cols], k_ref[:, cols], v_ref[:, cols]
        col = cum_t[:, h : h + 1]
        diff = jnp.minimum(col - cum[h : h + 1, :], 0.0)
        weight = jnp.where(causal, jnp.exp(diff), 0.0)
        probs = (dot(q, k, NT) * weight).astype(jnp.bfloat16)
        state = jnp.where(core == h // HALF, keep_ref[h % HALF], got_ref[h % HALF])
        mix = dot(probs, v, NN) + jnp.exp(col) * dot(q, state, NN)
        norm = lax.rsqrt(jnp.mean(mix * mix, axis=1, keepdims=True) + 1e-05)
        out_ref[:, cols] = (mix * norm * gain_ref[:, cols]).astype(jnp.bfloat16)


ROWS = HEADS * 64
KEYS = NY * NC * CH
SCALE = math.log2(math.e) / math.sqrt(DIM)


def softmax_kernel(*refs):
    q_ref = refs[0]
    pieces = refs[1:11]
    out_ref, kv_ref, qq_ref, s_ref, p_ref, pm_ref, al_ref, m_ref, acc_ref, sems = refs[11:]
    mx, my, mc = (lax.axis_index(a) for a in CTX)
    yc = my * NC + mc

    copies = []
    for n, ref in enumerate(pieces):
        other, part = divmod(n, 5)
        rows = pl.ds((other * 16 + (0, 4, 8, 12, 14)[part]) * CH, ref.shape[0])
        copies.append(pltpu.make_async_copy(ref, kv_ref.at[rows, :], sems.at[n]))
        copies[-1].start()

    def chunk(kx, k):
        other, i = divmod(k, 4)
        core = mc if other == 0 else 1 - mc
        d = (mx + NX - kx) % NX
        d = jnp.where(d < 2, d, 5 - d)
        slot = other * 16 + jnp.where(core == 0, i * 4 + d, d * 4 + i)
        y = (my + NY - (0, 1, 3, 2)[i]) % NY
        return pl.ds(pl.multiple_of(slot * CH, CH), CH), (y * NC + core) * CH

    for x in range(NX):
        for g in range(HEADS):
            rows = slice(x * ROWS + g * 64, x * ROWS + (g + 1) * 64)
            qq_ref[rows, :] = q_ref[x * 64 : (x + 1) * 64, g * DIM : (g + 1) * DIM]
    acc_ref[...] = jnp.zeros_like(acc_ref)
    for copy in copies:
        copy.wait()

    tiles = NX * (NX + 1) // 2

    def tile(t):
        t = jnp.int32(t)
        x = sum((t >= n).astype(jnp.int32) for n in (1, 3, 6))
        u = t - x * (x + 1) // 2
        return x, u, jnp.where(u == 0, x, u - 1), t % 2

    def scores(t):
        x, _, kx, slot = tile(t)
        r = lax.broadcasted_iota(jnp.int32, (ROWS, 1), 0) % 64
        pos = ((x - kx) * 8 + yc) * CH + (r // 8) * 32 + mx * 8 + r % 8
        qq = qq_ref[pl.ds(pl.multiple_of(x * ROWS, ROWS), ROWS), :]
        for k in range(KEYS // CH):
            rows, at = chunk(kx, k)
            s = dot(qq, kv_ref[rows, 0:DIM], NT) * SCALE
            lane = lax.broadcasted_iota(jnp.int32, s.shape, 1)
            s = jnp.where(lane <= pos - at, s, -1e30)
            s_ref[slot, :, k * CH : (k + 1) * CH] = s
            peak = jnp.maximum(s[:, :DIM], s[:, DIM:])
            if k > 0:
                peak = jnp.maximum(peak, pm_ref[slot])
            if k == KEYS // CH - 1:
                peak = jnp.broadcast_to(jnp.max(peak, axis=1, keepdims=True), (ROWS, DIM))
            pm_ref[slot] = peak

    def weights(t):
        _, u, _, slot = tile(t)
        for i in range(ROWS // 64):
            rows = slice(i * 64, (i + 1) * 64)
            old = jnp.where(u == 0, -1e30, m_ref[rows, :])
            new = jnp.maximum(old, pm_ref[slot, rows, :])
            al_ref[slot, rows, :] = jnp.exp2(old - new)
            m_ref[rows, :] = new
            for k in range(KEYS // DIM):
                cols = slice(k * DIM, (k + 1) * DIM)
                p_ref[slot, rows, cols] = jnp.exp2(s_ref[slot, rows, cols] - new).astype(
                    jnp.bfloat16
                )

    def mix(t):
        _, _, kx, slot = tile(t)
        values = [kv_ref[chunk(kx, k)[0], DIM : 2 * DIM] for k in range(KEYS // CH)]
        values = jnp.concatenate(values, axis=0)
        values = jnp.concatenate([values, jnp.ones_like(values)], axis=1)
        alpha = al_ref[slot]
        alpha = jnp.concatenate([alpha, alpha], axis=1)
        acc_ref[...] = acc_ref[...] * alpha + dot(p_ref[slot], values, NN)

    def finish(t):
        x, u, _, _ = tile(t)

        @pl.when(u == x)
        def _():
            for g in range(HEADS):
                rows = slice(g * 64, (g + 1) * 64)
                o = acc_ref[rows, 0:DIM] / acc_ref[rows, DIM : 2 * DIM]
                out_ref[pl.ds(pl.multiple_of(x * 64, 64), 64), g * DIM : (g + 1) * DIM] = o.astype(
                    jnp.bfloat16
                )

    scores(0)
    weights(0)
    scores(1)

    @pl.loop(0, tiles - 2)
    def _(t):
        mix(t)
        scores(t + 2)
        weights(t + 1)
        finish(t)

    mix(tiles - 2)
    weights(tiles - 1)
    mix(tiles - 1)
    finish(tiles - 1)


def vmem(n):
    return [pl.BlockSpec(memory_space=pltpu.VMEM)] * n


def call(kernel, outs, n, flops, **kw):
    return pl.pallas_call(
        kernel,
        out_shape=[jax.ShapeDtypeStruct(*o) for o in outs],
        in_specs=kw.pop("in_specs", vmem(n)),
        out_specs=vmem(len(outs)),
        compiler_params=pltpu.CompilerParams(vmem_limit_bytes=kw.pop("limit", 32 << 20)),
        cost_estimate=pl.CostEstimate(flops=flops, bytes_accessed=2 << 20, transcendentals=0),
        **kw,
    )


def ctx_index(x, y, c):
    return (x % NX * NY + y % NY) * NC + c


def ring(first, sign):
    pairs = []
    for x in range(NX):
        for y in range(NY):
            for c in range(NC):
                along_x = (c == 0) == first
                to = (x + sign, y) if along_x else (x, y + sign)
                pairs.append((ctx_index(x, y, c), ctx_index(*to, c)))
    return pairs


def permute(value, pairs, axes=CTX):
    return lax.ppermute(value, axes, pairs)


def exchange(value, axes):
    return lax.all_to_all(value, axes, 0, 0, tiled=True)


def gather_kv(own):
    r1 = permute(own, ring(True, 1))
    r2 = permute(own, ring(True, -1))
    r3 = permute(own, ring(True, 2))
    row = jnp.concatenate([own, r1, r2, r3], axis=0)
    s1 = permute(row, ring(False, 1))
    s2 = permute(row, ring(False, -1))
    t1 = permute(s1[: 2 * CH], ring(False, 1))
    t2 = permute(s2[2 * CH :], ring(False, -1))
    mine = [row, s1, s2, t1, t2]
    swap = [(0, 1), (1, 0)]
    return mine + [permute(p, swap, "ctx_2") for p in mine]


def both(lin_q, lin_k, lin_v, log_decay, lin_gain, soft_q, soft_kv):
    kv = soft_kv.reshape(32, NZ, 2 * DIM).swapaxes(0, 1)
    kv = exchange(kv, "head").reshape(CH, 2 * DIM)
    q = soft_q.reshape(NX, 8, NZ, HEADS * DIM).swapaxes(1, 2).reshape(NX * NZ, 8, HEADS * DIM)
    q = exchange(q, ("ctx_0", "head")).reshape(CH, HEADS * DIM)
    pieces = gather_kv(kv)

    swap = [(0, 1), (1, 0)]
    head = (DIM + TOTAL, DIM)
    heads = ((HALF, *head), jnp.bfloat16)
    one = (head, jnp.bfloat16)

    def send_y(values):
        return [
            permute(v, [(y, (y + d) % NY) for y in range(NY)], "ctx_1")
            for d, v in enumerate(values)
            if d > 0
        ]

    mine, theirs = call(local_state_kernel, [heads] * 2, 3, 1 << 28)(lin_k, lin_v, log_decay)
    other = permute(theirs, swap, "ctx_2")
    chip = call(chip_state_kernel, [one] * NY, 2, 1 << 20)(mine, other)
    row_state, before = call(
        row_state_kernel,
        [one, ((NY, DIM + 8, DIM), jnp.float32)],
        4,
        1 << 20,
        scratch_shapes=[pltpu.VMEM((NY, *head), jnp.bfloat16)],
    )(chip[0], *send_y(chip))
    earlier = [permute(row_state, [(x, x + d) for x in range(NX - d)], "ctx_0") for d in (1, 2, 3)]
    enter = call(enter_row_kernel, [((DIM, DIM), jnp.bfloat16)] * NY, 4, 1 << 20)(*earlier, before)
    entering = ((HALF, DIM, DIM), jnp.bfloat16)
    keep, send = call(enter_chunk_kernel, [entering] * 2, 6, 1 << 20)(
        enter[0], *send_y(enter), mine, other
    )
    got = permute(send, swap, "ctx_2")

    block = ((CH, HEADS * DIM), jnp.bfloat16)
    (soft,) = call(
        softmax_kernel,
        [block],
        11,
        1 << 34,
        in_specs=vmem(1) + [pl.BlockSpec(memory_space=pl.ANY)] * 10,
        limit=28 << 20,
        scratch_shapes=[
            pltpu.VMEM((NX * NY * NC * CH, 2 * DIM), jnp.bfloat16),
            pltpu.VMEM((NX * ROWS, DIM), jnp.bfloat16),
            pltpu.VMEM((2, ROWS, KEYS), jnp.float32),
            pltpu.VMEM((2, ROWS, KEYS), jnp.bfloat16),
            pltpu.VMEM((2, ROWS, DIM), jnp.float32),
            pltpu.VMEM((2, ROWS, DIM), jnp.float32),
            pltpu.VMEM((ROWS, DIM), jnp.float32),
            pltpu.VMEM((ROWS, 2 * DIM), jnp.float32),
            pltpu.SemaphoreType.DMA((10,)),
        ],
    )(q, *pieces)
    soft = exchange(soft.reshape(NX * NZ, 8, HEADS * DIM), ("ctx_0", "head"))
    soft_out = soft.reshape(NX, NZ, 8, HEADS * DIM).swapaxes(1, 2).reshape(32, NZ * HEADS * DIM)

    (lin_out,) = call(lightning_kernel, [block], 7, 1 << 29)(
        lin_q, lin_k, lin_v, log_decay, lin_gain.reshape(1, -1), keep, got
    )
    return (lin_out, soft_out)


def solution(mesh):
    finer = Mesh(
        mesh.devices.reshape(NX, NY, NC, NZ), ("ctx_0", "ctx_1", "ctx_2", "head")
    )
    placed = (
        P(CTX, "head"),
        P(CTX, "head"),
        P(CTX, "head"),
        P("head", CTX),
        P("head"),
        P(CTX_HEAD, None),
        P(CTX_HEAD, None),
    )
    return jax.shard_map(
        both,
        mesh=finer,
        in_specs=placed,
        out_specs=(P(CTX, "head"), P(CTX_HEAD, None)),
        check_vma=False,
    )
```

```python
import math

import jax
import jax.numpy as jnp
from jax import lax
from jax.experimental import pallas as pl
from jax.experimental.pallas import tpu as pltpu
from jax.sharding import Mesh
from jax.sharding import PartitionSpec as P

CTX = ("ctx_0", "ctx_1", "ctx_2")
CTX_HEAD = ("ctx_0", "ctx_1", "ctx_2", "head")
NX, NY, NC, NZ = 4, 4, 2, 8
CH = 256
DIM = 128
HEADS = 8
HALF = HEADS // 2
TOTAL = 16

NT = (((1,), (1,)), ((), ()))
NN = (((1,), (0,)), ((), ()))
TN = (((0,), (0,)), ((), ()))


def dot(a, b, dims):
    return lax.dot_general(a, b, dims, preferred_element_type=jnp.float32)


def running_sum(g):
    lane = lax.broadcasted_iota(jnp.int32, g.shape, 1)
    step = 1
    while step < g.shape[1]:
        g = g + jnp.where(lane >= step, pltpu.roll(g, step, 1), 0.0)
        step *= 2
    return g


def columns(cum):
    wide = jnp.concatenate([cum, jnp.zeros((DIM - cum.shape[0], cum.shape[1]), cum.dtype)], 0)
    return wide.T


def total_rows(total):
    row = lax.broadcasted_iota(jnp.int32, (TOTAL, DIM), 0)
    total = jnp.broadcast_to(total, (TOTAL, DIM))
    high = total.astype(jnp.bfloat16).astype(jnp.float32)
    return jnp.where(row == 0, high, jnp.where(row == 1, total - high, 0.0)).astype(jnp.bfloat16)


def read_total(ref):
    rows = ref[DIM : DIM + TOTAL, :].astype(jnp.float32)
    return rows[0:1] + rows[1:2]


def read_state(ref):
    return ref[0:DIM, :].astype(jnp.float32)


def write(ref, state, total):
    ref[0:DIM, :] = state.astype(jnp.bfloat16)
    ref[DIM : DIM + TOTAL, :] = total_rows(total)


def local_state_kernel(k_ref, v_ref, g_ref, mine_ref, theirs_ref):
    first = lax.axis_index("ctx_2") == 0
    cum = running_sum(g_ref[...])
    cum_t = columns(cum)

    def local(h):
        cols = slice(h * DIM, (h + 1) * DIM)
        last = cum[h : h + 1, CH - 1 : CH]
        scale = jnp.exp(last - cum_t[:, h : h + 1])
        ks = (k_ref[:, cols].astype(jnp.float32) * scale).astype(jnp.bfloat16)
        return dot(ks, v_ref[:, cols], TN), last

    for h in range(HALF):
        low, low_total = local(h)
        high, high_total = local(HALF + h)
        write(
            mine_ref.at[h], jnp.where(first, low, high), jnp.where(first, low_total, high_total)
        )
        write(
            theirs_ref.at[h], jnp.where(first, high, low), jnp.where(first, high_total, low_total)
        )


def in_order(first, mine_ref, other_ref):
    a, b = read_state(mine_ref), read_state(other_ref)
    ta, tb = read_total(mine_ref), read_total(other_ref)
    return (
        jnp.where(first, a, b),
        jnp.where(first, ta, tb),
        jnp.where(first, b, a),
        jnp.where(first, tb, ta),
    )


def chip_state_kernel(mine_ref, other_ref, *chip_refs):
    my, first = lax.axis_index("ctx_1"), lax.axis_index("ctx_2") == 0
    for d, chip_ref in enumerate(chip_refs):
        h = (my + d) % NY
        s0, t0, s1, t1 = in_order(first, mine_ref.at[h], other_ref.at[h])
        write(chip_ref, jnp.exp(t1) * s0 + s1, t0 + t1)


def row_state_kernel(own_ref, a_ref, b_ref, c_ref, row_ref, before_ref, all_ref):
    my = lax.axis_index("ctx_1")
    for d, ref in enumerate((own_ref, a_ref, b_ref, c_ref)):
        all_ref[(my + NY - d) % NY] = ref[...]
    state = jnp.zeros((DIM, DIM), jnp.float32)
    total = jnp.zeros((1, DIM), jnp.float32)
    for y in range(NY):
        before_ref[y, 0:DIM, :] = state
        before_ref[y, DIM : DIM + 8, :] = jnp.broadcast_to(total, (8, DIM))
        t = read_total(all_ref.at[y])
        state = jnp.exp(t) * state + read_state(all_ref.at[y])
        total = total + t
    write(row_ref, state, total)


def enter_row_kernel(a_ref, b_ref, c_ref, before_ref, *out_refs):
    mx, my = lax.axis_index("ctx_0"), lax.axis_index("ctx_1")
    state = jnp.zeros((DIM, DIM), jnp.float32)
    for d, ref in ((3, c_ref), (2, b_ref), (1, a_ref)):
        new = jnp.exp(read_total(ref)) * state + read_state(ref)
        state = jnp.where(mx >= d, new, state)
    for d, out_ref in enumerate(out_refs):
        y = (my + d) % NY
        before = before_ref[y]
        out = jnp.exp(before[DIM : DIM + 1]) * state + before[0:DIM]
        out_ref[...] = out.astype(jnp.bfloat16)


def enter_chunk_kernel(e0_ref, e1_ref, e2_ref, e3_ref, mine_ref, other_ref, keep_ref, send_ref):
    my, first = lax.axis_index("ctx_1"), lax.axis_index("ctx_2") == 0
    for d, ref in enumerate((e0_ref, e1_ref, e2_ref, e3_ref)):
        h = (my + NY - d) % NY
        state = ref[...].astype(jnp.float32)
        s0, t0, _, _ = in_order(first, mine_ref.at[h], other_ref.at[h])
        later = jnp.exp(t0) * state + s0
        keep_ref[h] = jnp.where(first, state, later).astype(jnp.bfloat16)
        send_ref[h] = jnp.where(first, later, state).astype(jnp.bfloat16)


def lightning_kernel(q_ref, k_ref, v_ref, g_ref, gain_ref, keep_ref, got_ref, out_ref):
    core = lax.axis_index("ctx_2")
    cum = running_sum(g_ref[...])
    cum_t = columns(cum)
    causal = lax.broadcasted_iota(jnp.int32, (CH, CH), 0) >= lax.broadcasted_iota(
        jnp.int32, (CH, CH), 1
    )
    for h in range(HEADS):
        cols = slice(h * DIM, (h + 1) * DIM)
        q, k, v = q_ref[:, cols], k_ref[:, cols], v_ref[:, cols]
        col = cum_t[:, h : h + 1]
        diff = jnp.minimum(col - cum[h : h + 1, :], 0.0)
        weight = jnp.where(causal, jnp.exp(diff), 0.0)
        probs = (dot(q, k, NT) * weight).astype(jnp.bfloat16)
        state = jnp.where(core == h // HALF, keep_ref[h % HALF], got_ref[h % HALF])
        mix = dot(probs, v, NN) + jnp.exp(col) * dot(q, state, NN)
        norm = lax.rsqrt(jnp.mean(mix * mix, axis=1, keepdims=True) + 1e-05)
        out_ref[:, cols] = (mix * norm * gain_ref[:, cols]).astype(jnp.bfloat16)


def cut_kernel(kv_ref, *out_refs):
    mz = lax.axis_index("head")
    for d, out_ref in enumerate(out_refs):
        z = (mz + d) % NZ
        out_ref[...] = kv_ref[:, pl.ds(pl.multiple_of(z * 2 * DIM, 2 * DIM), 2 * DIM)]


def join_kernel(*refs):
    mz = lax.axis_index("head")
    out_ref = refs[-1]
    for d, ref in enumerate(refs[:-1]):
        z = (mz + NZ - d) % NZ
        out_ref[pl.ds(pl.multiple_of(z * 32, 32), 32), :] = ref[...]


ROWS = HEADS * 64
KEYS = NY * NC * CH
SCALE = math.log2(math.e) / math.sqrt(DIM)


def softmax_kernel(*refs):
    q_ref = refs[0]
    pieces = refs[1:11]
    out_ref, kv_ref, qq_ref, s_ref, p_ref, pm_ref, al_ref, m_ref, acc_ref, sems = refs[11:]
    mx, my, mc = (lax.axis_index(a) for a in CTX)
    yc = my * NC + mc

    copies = []
    for n, ref in enumerate(pieces):
        other, part = divmod(n, 5)
        rows = pl.ds((other * 16 + (0, 4, 8, 12, 14)[part]) * CH, ref.shape[0])
        copies.append(pltpu.make_async_copy(ref, kv_ref.at[rows, :], sems.at[n]))
        copies[-1].start()

    def chunk(kx, k):
        other, i = divmod(k, 4)
        core = mc if other == 0 else 1 - mc
        d = (mx + NX - kx) % NX
        d = jnp.where(d < 2, d, 5 - d)
        slot = other * 16 + jnp.where(core == 0, i * 4 + d, d * 4 + i)
        y = (my + NY - (0, 1, 3, 2)[i]) % NY
        return pl.ds(pl.multiple_of(slot * CH, CH), CH), (y * NC + core) * CH

    for x in range(NX):
        for g in range(HEADS):
            rows = slice(x * ROWS + g * 64, x * ROWS + (g + 1) * 64)
            qq_ref[rows, :] = q_ref[x * 64 : (x + 1) * 64, g * DIM : (g + 1) * DIM]
    acc_ref[...] = jnp.zeros_like(acc_ref)
    for copy in copies:
        copy.wait()

    tiles = NX * (NX + 1) // 2

    def tile(t):
        t = jnp.int32(t)
        x = sum((t >= n).astype(jnp.int32) for n in (1, 3, 6))
        u = t - x * (x + 1) // 2
        return x, u, jnp.where(u == 0, x, u - 1), t % 2

    def scores(t):
        x, _, kx, slot = tile(t)
        r = lax.broadcasted_iota(jnp.int32, (ROWS, 1), 0) % 64
        pos = ((x - kx) * 8 + yc) * CH + (r // 8) * 32 + mx * 8 + r % 8
        qq = qq_ref[pl.ds(pl.multiple_of(x * ROWS, ROWS), ROWS), :]
        for k in range(KEYS // CH):
            rows, at = chunk(kx, k)
            s = dot(qq, kv_ref[rows, 0:DIM], NT) * SCALE
            lane = lax.broadcasted_iota(jnp.int32, s.shape, 1)
            s = jnp.where(lane <= pos - at, s, -1e30)
            s_ref[slot, :, k * CH : (k + 1) * CH] = s
            peak = jnp.maximum(s[:, :DIM], s[:, DIM:])
            if k > 0:
                peak = jnp.maximum(peak, pm_ref[slot])
            if k == KEYS // CH - 1:
                peak = jnp.broadcast_to(jnp.max(peak, axis=1, keepdims=True), (ROWS, DIM))
            pm_ref[slot] = peak

    def weights(t):
        _, u, _, slot = tile(t)
        for i in range(ROWS // 64):
            rows = slice(i * 64, (i + 1) * 64)
            old = jnp.where(u == 0, -1e30, m_ref[rows, :])
            new = jnp.maximum(old, pm_ref[slot, rows, :])
            al_ref[slot, rows, :] = jnp.exp2(old - new)
            m_ref[rows, :] = new
            for k in range(KEYS // DIM):
                cols = slice(k * DIM, (k + 1) * DIM)
                p_ref[slot, rows, cols] = jnp.exp2(s_ref[slot, rows, cols] - new).astype(
                    jnp.bfloat16
                )

    def mix(t):
        _, _, kx, slot = tile(t)
        values = [kv_ref[chunk(kx, k)[0], DIM : 2 * DIM] for k in range(KEYS // CH)]
        values = jnp.concatenate(values, axis=0)
        values = jnp.concatenate([values, jnp.ones_like(values)], axis=1)
        alpha = al_ref[slot]
        alpha = jnp.concatenate([alpha, alpha], axis=1)
        acc_ref[...] = acc_ref[...] * alpha + dot(p_ref[slot], values, NN)

    def finish(t):
        x, u, _, _ = tile(t)

        @pl.when(u == x)
        def _():
            for g in range(HEADS):
                rows = slice(g * 64, (g + 1) * 64)
                o = acc_ref[rows, 0:DIM] / acc_ref[rows, DIM : 2 * DIM]
                out_ref[pl.ds(pl.multiple_of(x * 64, 64), 64), g * DIM : (g + 1) * DIM] = o.astype(
                    jnp.bfloat16
                )

    scores(0)
    weights(0)
    scores(1)

    @pl.loop(0, tiles - 2)
    def _(t):
        mix(t)
        scores(t + 2)
        weights(t + 1)
        finish(t)

    mix(tiles - 2)
    weights(tiles - 1)
    mix(tiles - 1)
    finish(tiles - 1)


def vmem(n):
    return [pl.BlockSpec(memory_space=pltpu.VMEM)] * n


def call(kernel, outs, n, flops, **kw):
    return pl.pallas_call(
        kernel,
        out_shape=[jax.ShapeDtypeStruct(*o) for o in outs],
        in_specs=kw.pop("in_specs", vmem(n)),
        out_specs=vmem(len(outs)),
        compiler_params=pltpu.CompilerParams(vmem_limit_bytes=kw.pop("limit", 32 << 20)),
        cost_estimate=pl.CostEstimate(flops=flops, bytes_accessed=2 << 20, transcendentals=0),
        **kw,
    )


def ctx_index(x, y, c):
    return (x % NX * NY + y % NY) * NC + c


def ring(first, sign):
    pairs = []
    for x in range(NX):
        for y in range(NY):
            for c in range(NC):
                along_x = (c == 0) == first
                to = (x + sign, y) if along_x else (x, y + sign)
                pairs.append((ctx_index(x, y, c), ctx_index(*to, c)))
    return pairs


def permute(value, pairs, axes=CTX):
    return lax.ppermute(value, axes, pairs)


def exchange(value, axes):
    return lax.all_to_all(value, axes, 0, 0, tiled=True)


def gather_kv(own):
    r1 = permute(own, ring(True, 1))
    r2 = permute(own, ring(True, -1))
    r3 = permute(own, ring(True, 2))
    row = jnp.concatenate([own, r1, r2, r3], axis=0)
    s1 = permute(row, ring(False, 1))
    s2 = permute(row, ring(False, -1))
    t1 = permute(s1[: 2 * CH], ring(False, 1))
    t2 = permute(s2[2 * CH :], ring(False, -1))
    mine = [row, s1, s2, t1, t2]
    swap = [(0, 1), (1, 0)]
    return mine + [permute(p, swap, "ctx_2") for p in mine]


def both(lin_q, lin_k, lin_v, log_decay, lin_gain, soft_q, soft_kv):
    part = ((32, 2 * DIM), jnp.bfloat16)
    parts = call(cut_kernel, [part] * NZ, 1, 1 << 18)(soft_kv)
    parts = [parts[0]] + [
        permute(parts[d], [(z, (z + d) % NZ) for z in range(NZ)], "head")
        for d in range(1, NZ)
    ]
    (kv,) = call(join_kernel, [((CH, 2 * DIM), jnp.bfloat16)], NZ, 1 << 18)(*parts)
    q = soft_q.reshape(NX, 8, NZ, HEADS * DIM).swapaxes(1, 2).reshape(NX * NZ, 8, HEADS * DIM)
    q = exchange(q, ("ctx_0", "head")).reshape(CH, HEADS * DIM)
    pieces = gather_kv(kv)

    swap = [(0, 1), (1, 0)]
    head = (DIM + TOTAL, DIM)
    heads = ((HALF, *head), jnp.bfloat16)
    one = (head, jnp.bfloat16)

    def send_y(values):
        return [
            permute(v, [(y, (y + d) % NY) for y in range(NY)], "ctx_1")
            for d, v in enumerate(values)
            if d > 0
        ]

    mine, theirs = call(local_state_kernel, [heads] * 2, 3, 1 << 28)(lin_k, lin_v, log_decay)
    other = permute(theirs, swap, "ctx_2")
    chip = call(chip_state_kernel, [one] * NY, 2, 1 << 20)(mine, other)
    row_state, before = call(
        row_state_kernel,
        [one, ((NY, DIM + 8, DIM), jnp.float32)],
        4,
        1 << 20,
        scratch_shapes=[pltpu.VMEM((NY, *head), jnp.bfloat16)],
    )(chip[0], *send_y(chip))
    earlier = [permute(row_state, [(x, x + d) for x in range(NX - d)], "ctx_0") for d in (1, 2, 3)]
    enter = call(enter_row_kernel, [((DIM, DIM), jnp.bfloat16)] * NY, 4, 1 << 20)(*earlier, before)
    entering = ((HALF, DIM, DIM), jnp.bfloat16)
    keep, send = call(enter_chunk_kernel, [entering] * 2, 6, 1 << 20)(
        enter[0], *send_y(enter), mine, other
    )
    got = permute(send, swap, "ctx_2")

    block = ((CH, HEADS * DIM), jnp.bfloat16)
    (soft,) = call(
        softmax_kernel,
        [block],
        11,
        1 << 34,
        in_specs=vmem(1) + [pl.BlockSpec(memory_space=pl.ANY)] * 10,
        limit=28 << 20,
        scratch_shapes=[
            pltpu.VMEM((NX * NY * NC * CH, 2 * DIM), jnp.bfloat16),
            pltpu.VMEM((NX * ROWS, DIM), jnp.bfloat16),
            pltpu.VMEM((2, ROWS, KEYS), jnp.float32),
            pltpu.VMEM((2, ROWS, KEYS), jnp.bfloat16),
            pltpu.VMEM((2, ROWS, DIM), jnp.float32),
            pltpu.VMEM((2, ROWS, DIM), jnp.float32),
            pltpu.VMEM((ROWS, DIM), jnp.float32),
            pltpu.VMEM((ROWS, 2 * DIM), jnp.float32),
            pltpu.SemaphoreType.DMA((10,)),
        ],
    )(q, *pieces)
    soft = exchange(soft.reshape(NX * NZ, 8, HEADS * DIM), ("ctx_0", "head"))
    soft_out = soft.reshape(NX, NZ, 8, HEADS * DIM).swapaxes(1, 2).reshape(32, NZ * HEADS * DIM)

    (lin_out,) = call(lightning_kernel, [block], 7, 1 << 29)(
        lin_q, lin_k, lin_v, log_decay, lin_gain.reshape(1, -1), keep, got
    )
    return (lin_out, soft_out)


def solution(mesh):
    finer = Mesh(
        mesh.devices.reshape(NX, NY, NC, NZ), ("ctx_0", "ctx_1", "ctx_2", "head")
    )
    placed = (
        P(CTX, "head"),
        P(CTX, "head"),
        P(CTX, "head"),
        P("head", CTX),
        P("head"),
        P(CTX_HEAD, None),
        P(CTX_HEAD, None),
    )
    return jax.shard_map(
        both,
        mesh=finer,
        in_specs=placed,
        out_specs=(P(CTX, "head"), P(CTX_HEAD, None)),
        check_vma=False,
    )
```

```python
import math

import jax
import jax.numpy as jnp
from jax import lax
from jax.experimental import pallas as pl
from jax.experimental.pallas import tpu as pltpu
from jax.sharding import Mesh
from jax.sharding import PartitionSpec as P

CTX = ("ctx_0", "ctx_1", "ctx_2")
CTX_HEAD = ("ctx_0", "ctx_1", "ctx_2", "head")
NX, NY, NC, NZ = 4, 4, 2, 8
CH = 256
DIM = 128
HEADS = 8
HALF = HEADS // 2
TOTAL = 16

NT = (((1,), (1,)), ((), ()))
NN = (((1,), (0,)), ((), ()))
TN = (((0,), (0,)), ((), ()))


def dot(a, b, dims):
    return lax.dot_general(a, b, dims, preferred_element_type=jnp.float32)


def running_sum(g):
    lane = lax.broadcasted_iota(jnp.int32, g.shape, 1)
    step = 1
    while step < g.shape[1]:
        g = g + jnp.where(lane >= step, pltpu.roll(g, step, 1), 0.0)
        step *= 2
    return g


def columns(cum):
    wide = jnp.concatenate([cum, jnp.zeros((DIM - cum.shape[0], cum.shape[1]), cum.dtype)], 0)
    return wide.T


def total_rows(total):
    row = lax.broadcasted_iota(jnp.int32, (TOTAL, DIM), 0)
    total = jnp.broadcast_to(total, (TOTAL, DIM))
    high = total.astype(jnp.bfloat16).astype(jnp.float32)
    return jnp.where(row == 0, high, jnp.where(row == 1, total - high, 0.0)).astype(jnp.bfloat16)


def read_total(ref):
    rows = ref[DIM : DIM + TOTAL, :].astype(jnp.float32)
    return rows[0:1] + rows[1:2]


def read_state(ref):
    return ref[0:DIM, :].astype(jnp.float32)


def write(ref, state, total):
    ref[0:DIM, :] = state.astype(jnp.bfloat16)
    ref[DIM : DIM + TOTAL, :] = total_rows(total)


def local_state_kernel(k_ref, v_ref, g_ref, mine_ref, theirs_ref):
    first = lax.axis_index("ctx_2") == 0
    cum = running_sum(g_ref[...])
    cum_t = columns(cum)

    def local(h):
        cols = slice(h * DIM, (h + 1) * DIM)
        last = cum[h : h + 1, CH - 1 : CH]
        scale = jnp.exp(last - cum_t[:, h : h + 1])
        ks = (k_ref[:, cols].astype(jnp.float32) * scale).astype(jnp.bfloat16)
        return dot(ks, v_ref[:, cols], TN), last

    for h in range(HALF):
        low, low_total = local(h)
        high, high_total = local(HALF + h)
        write(
            mine_ref.at[h], jnp.where(first, low, high), jnp.where(first, low_total, high_total)
        )
        write(
            theirs_ref.at[h], jnp.where(first, high, low), jnp.where(first, high_total, low_total)
        )


def in_order(first, mine_ref, other_ref):
    a, b = read_state(mine_ref), read_state(other_ref)
    ta, tb = read_total(mine_ref), read_total(other_ref)
    return (
        jnp.where(first, a, b),
        jnp.where(first, ta, tb),
        jnp.where(first, b, a),
        jnp.where(first, tb, ta),
    )


def chip_state_kernel(mine_ref, other_ref, *chip_refs):
    my, first = lax.axis_index("ctx_1"), lax.axis_index("ctx_2") == 0
    for d, chip_ref in enumerate(chip_refs):
        h = (my + d) % NY
        s0, t0, s1, t1 = in_order(first, mine_ref.at[h], other_ref.at[h])
        write(chip_ref, jnp.exp(t1) * s0 + s1, t0 + t1)


def row_state_kernel(own_ref, a_ref, b_ref, c_ref, row_ref, before_ref, all_ref):
    my = lax.axis_index("ctx_1")
    for d, ref in enumerate((own_ref, a_ref, b_ref, c_ref)):
        all_ref[(my + NY - d) % NY] = ref[...]
    state = jnp.zeros((DIM, DIM), jnp.float32)
    total = jnp.zeros((1, DIM), jnp.float32)
    for y in range(NY):
        before_ref[y, 0:DIM, :] = state
        before_ref[y, DIM : DIM + 8, :] = jnp.broadcast_to(total, (8, DIM))
        t = read_total(all_ref.at[y])
        state = jnp.exp(t) * state + read_state(all_ref.at[y])
        total = total + t
    write(row_ref, state, total)


def enter_row_kernel(a_ref, b_ref, c_ref, before_ref, *out_refs):
    mx, my = lax.axis_index("ctx_0"), lax.axis_index("ctx_1")
    state = jnp.zeros((DIM, DIM), jnp.float32)
    for d, ref in ((3, c_ref), (2, b_ref), (1, a_ref)):
        new = jnp.exp(read_total(ref)) * state + read_state(ref)
        state = jnp.where(mx >= d, new, state)
    for d, out_ref in enumerate(out_refs):
        y = (my + d) % NY
        before = before_ref[y]
        out = jnp.exp(before[DIM : DIM + 1]) * state + before[0:DIM]
        out_ref[...] = out.astype(jnp.bfloat16)


def enter_chunk_kernel(e0_ref, e1_ref, e2_ref, e3_ref, mine_ref, other_ref, keep_ref, send_ref):
    my, first = lax.axis_index("ctx_1"), lax.axis_index("ctx_2") == 0
    for d, ref in enumerate((e0_ref, e1_ref, e2_ref, e3_ref)):
        h = (my + NY - d) % NY
        state = ref[...].astype(jnp.float32)
        s0, t0, _, _ = in_order(first, mine_ref.at[h], other_ref.at[h])
        later = jnp.exp(t0) * state + s0
        keep_ref[h] = jnp.where(first, state, later).astype(jnp.bfloat16)
        send_ref[h] = jnp.where(first, later, state).astype(jnp.bfloat16)


def lightning_kernel(q_ref, k_ref, v_ref, g_ref, gain_ref, keep_ref, got_ref, out_ref):
    core = lax.axis_index("ctx_2")
    cum = running_sum(g_ref[...])
    cum_t = columns(cum)
    causal = lax.broadcasted_iota(jnp.int32, (CH, CH), 0) >= lax.broadcasted_iota(
        jnp.int32, (CH, CH), 1
    )
    for h in range(HEADS):
        cols = slice(h * DIM, (h + 1) * DIM)
        q, k, v = q_ref[:, cols], k_ref[:, cols], v_ref[:, cols]
        col = cum_t[:, h : h + 1]
        diff = jnp.minimum(col - cum[h : h + 1, :], 0.0)
        weight = jnp.where(causal, jnp.exp(diff), 0.0)
        probs = (dot(q, k, NT) * weight).astype(jnp.bfloat16)
        state = jnp.where(core == h // HALF, keep_ref[h % HALF], got_ref[h % HALF])
        mix = dot(probs, v, NN) + jnp.exp(col) * dot(q, state, NN)
        norm = lax.rsqrt(jnp.mean(mix * mix, axis=1, keepdims=True) + 1e-05)
        out_ref[:, cols] = (mix * norm * gain_ref[:, cols]).astype(jnp.bfloat16)


ROWS = HEADS * 64
KEYS = NY * NC * CH
SCALE = math.log2(math.e) / math.sqrt(DIM)


def softmax_kernel(*refs):
    q_ref = refs[0]
    pieces = refs[1:11]
    out_ref, kv_ref, qq_ref, s_ref, p_ref, pm_ref, al_ref, m_ref, acc_ref, sems = refs[11:]
    mx, my, mc = (lax.axis_index(a) for a in CTX)
    yc = my * NC + mc

    def copies_of(parts):
        found = []
        for other in range(2):
            for part, at, size in parts:
                ref = pieces[5 * other + part]
                to = other * 16 + (0, 4, 8, 12, 14)[part] + at
                n = other * 8 + len(found) % 4 + (0 if parts is first_parts else 4)
                found.append(
                    pltpu.make_async_copy(
                        ref.at[pl.ds(at * CH, size * CH), :],
                        kv_ref.at[pl.ds(to * CH, size * CH), :],
                        sems.at[n],
                    )
                )
        for copy in found:
            copy.start()
        return found

    first_parts = ((0, 0, 4), (1, 0, 1), (2, 0, 1), (3, 0, 1))
    first_copies = copies_of(first_parts)
    other_copies = copies_of(((1, 1, 3), (2, 1, 3), (3, 1, 1), (4, 0, 2)))

    def chunk(kx, k):
        other, i = divmod(k, 4)
        core = mc if other == 0 else 1 - mc
        d = (mx + NX - kx) % NX
        d = jnp.where(d < 2, d, 5 - d)
        slot = other * 16 + jnp.where(core == 0, i * 4 + d, d * 4 + i)
        y = (my + NY - (0, 1, 3, 2)[i]) % NY
        return pl.ds(pl.multiple_of(slot * CH, CH), CH), (y * NC + core) * CH

    for x in range(NX):
        for g in range(HEADS):
            rows = slice(x * ROWS + g * 64, x * ROWS + (g + 1) * 64)
            qq_ref[rows, :] = q_ref[x * 64 : (x + 1) * 64, g * DIM : (g + 1) * DIM]
    acc_ref[...] = jnp.zeros_like(acc_ref)

    starts = [jnp.int32(0)]
    for i in range(NX - 1):
        starts.append(starts[-1] + (mx + i) % NX + 1)
    tiles = NX * (NX + 1) // 2

    def tile(t):
        t = jnp.int32(t)
        x, begin = mx, starts[0]
        for i in range(1, NX):
            x = jnp.where(t >= starts[i], (mx + i) % NX, x)
            begin = jnp.where(t >= starts[i], starts[i], begin)
        u = t - begin
        return x, u, jnp.where(u == 0, x, u - 1), t % 2

    def scores(t):
        x, _, kx, slot = tile(t)
        r = lax.broadcasted_iota(jnp.int32, (ROWS, 1), 0) % 64
        pos = ((x - kx) * 8 + yc) * CH + (r // 8) * 32 + mx * 8 + r % 8
        qq = qq_ref[pl.ds(pl.multiple_of(x * ROWS, ROWS), ROWS), :]
        for k in range(KEYS // CH):
            rows, at = chunk(kx, k)
            s = dot(qq, kv_ref[rows, 0:DIM], NT) * SCALE
            lane = lax.broadcasted_iota(jnp.int32, s.shape, 1)
            s = jnp.where(lane <= pos - at, s, -1e30)
            s_ref[slot, :, k * CH : (k + 1) * CH] = s
            peak = jnp.maximum(s[:, :DIM], s[:, DIM:])
            if k > 0:
                peak = jnp.maximum(peak, pm_ref[slot])
            if k == KEYS // CH - 1:
                peak = jnp.broadcast_to(jnp.max(peak, axis=1, keepdims=True), (ROWS, DIM))
            pm_ref[slot] = peak

    def weights(t):
        _, u, _, slot = tile(t)
        for i in range(ROWS // 64):
            rows = slice(i * 64, (i + 1) * 64)
            old = jnp.where(u == 0, -1e30, m_ref[rows, :])
            new = jnp.maximum(old, pm_ref[slot, rows, :])
            al_ref[slot, rows, :] = jnp.exp2(old - new)
            m_ref[rows, :] = new
            for k in range(KEYS // DIM):
                cols = slice(k * DIM, (k + 1) * DIM)
                p_ref[slot, rows, cols] = jnp.exp2(s_ref[slot, rows, cols] - new).astype(
                    jnp.bfloat16
                )

    def mix(t):
        _, _, kx, slot = tile(t)
        values = [kv_ref[chunk(kx, k)[0], DIM : 2 * DIM] for k in range(KEYS // CH)]
        values = jnp.concatenate(values, axis=0)
        values = jnp.concatenate([values, jnp.ones_like(values)], axis=1)
        alpha = al_ref[slot]
        alpha = jnp.concatenate([alpha, alpha], axis=1)
        acc_ref[...] = acc_ref[...] * alpha + dot(p_ref[slot], values, NN)

    def finish(t):
        x, u, _, _ = tile(t)

        @pl.when(u == x)
        def _():
            for g in range(HEADS):
                rows = slice(g * 64, (g + 1) * 64)
                o = acc_ref[rows, 0:DIM] / acc_ref[rows, DIM : 2 * DIM]
                out_ref[pl.ds(pl.multiple_of(x * 64, 64), 64), g * DIM : (g + 1) * DIM] = o.astype(
                    jnp.bfloat16
                )

    for copy in first_copies:
        copy.wait()
    scores(0)
    weights(0)
    for copy in other_copies:
        copy.wait()
    scores(1)

    @pl.loop(0, tiles - 2)
    def _(t):
        mix(t)
        scores(t + 2)
        weights(t + 1)
        finish(t)

    mix(tiles - 2)
    weights(tiles - 1)
    finish(tiles - 2)
    mix(tiles - 1)
    finish(tiles - 1)


def vmem(n):
    return [pl.BlockSpec(memory_space=pltpu.VMEM)] * n


def call(kernel, outs, n, flops, **kw):
    return pl.pallas_call(
        kernel,
        out_shape=[jax.ShapeDtypeStruct(*o) for o in outs],
        in_specs=kw.pop("in_specs", vmem(n)),
        out_specs=vmem(len(outs)),
        compiler_params=pltpu.CompilerParams(vmem_limit_bytes=kw.pop("limit", 32 << 20)),
        cost_estimate=pl.CostEstimate(flops=flops, bytes_accessed=2 << 20, transcendentals=0),
        **kw,
    )


def ctx_index(x, y, c):
    return (x % NX * NY + y % NY) * NC + c


def ring(first, sign):
    pairs = []
    for x in range(NX):
        for y in range(NY):
            for c in range(NC):
                along_x = (c == 0) == first
                to = (x + sign, y) if along_x else (x, y + sign)
                pairs.append((ctx_index(x, y, c), ctx_index(*to, c)))
    return pairs


def permute(value, pairs, axes=CTX):
    return lax.ppermute(value, axes, pairs)


def exchange(value, axes):
    return lax.all_to_all(value, axes, 0, 0, tiled=True)


def gather_kv(own):
    r1 = permute(own, ring(True, 1))
    r2 = permute(own, ring(True, -1))
    r3 = permute(own, ring(True, 2))
    row = jnp.concatenate([own, r1, r2, r3], axis=0)
    s1 = permute(row, ring(False, 1))
    s2 = permute(row, ring(False, -1))
    t1 = permute(s1[: 2 * CH], ring(False, 1))
    t2 = permute(s2[2 * CH :], ring(False, -1))
    mine = [row, s1, s2, t1, t2]
    swap = [(0, 1), (1, 0)]
    return mine + [permute(p, swap, "ctx_2") for p in mine]


def both(lin_q, lin_k, lin_v, log_decay, lin_gain, soft_q, soft_kv):
    kv = soft_kv.reshape(32, NZ, 2 * DIM).swapaxes(0, 1)
    kv = exchange(kv, "head").reshape(CH, 2 * DIM)
    q = soft_q.reshape(NX, 8, NZ, HEADS * DIM).swapaxes(1, 2).reshape(NX * NZ, 8, HEADS * DIM)
    q = exchange(q, ("ctx_0", "head")).reshape(CH, HEADS * DIM)
    pieces = gather_kv(kv)

    swap = [(0, 1), (1, 0)]
    head = (DIM + TOTAL, DIM)
    heads = ((HALF, *head), jnp.bfloat16)
    one = (head, jnp.bfloat16)

    def send_y(values):
        return [
            permute(v, [(y, (y + d) % NY) for y in range(NY)], "ctx_1")
            for d, v in enumerate(values)
            if d > 0
        ]

    mine, theirs = call(local_state_kernel, [heads] * 2, 3, 1 << 28)(lin_k, lin_v, log_decay)
    other = permute(theirs, swap, "ctx_2")
    chip = call(chip_state_kernel, [one] * NY, 2, 1 << 20)(mine, other)
    row_state, before = call(
        row_state_kernel,
        [one, ((NY, DIM + 8, DIM), jnp.float32)],
        4,
        1 << 20,
        scratch_shapes=[pltpu.VMEM((NY, *head), jnp.bfloat16)],
    )(chip[0], *send_y(chip))
    earlier = [permute(row_state, [(x, x + d) for x in range(NX - d)], "ctx_0") for d in (1, 2, 3)]
    enter = call(enter_row_kernel, [((DIM, DIM), jnp.bfloat16)] * NY, 4, 1 << 20)(*earlier, before)
    entering = ((HALF, DIM, DIM), jnp.bfloat16)
    keep, send = call(enter_chunk_kernel, [entering] * 2, 6, 1 << 20)(
        enter[0], *send_y(enter), mine, other
    )
    got = permute(send, swap, "ctx_2")

    block = ((CH, HEADS * DIM), jnp.bfloat16)
    (soft,) = call(
        softmax_kernel,
        [block],
        11,
        1 << 34,
        in_specs=vmem(1) + [pl.BlockSpec(memory_space=pl.ANY)] * 10,
        limit=28 << 20,
        scratch_shapes=[
            pltpu.VMEM((NX * NY * NC * CH, 2 * DIM), jnp.bfloat16),
            pltpu.VMEM((NX * ROWS, DIM), jnp.bfloat16),
            pltpu.VMEM((2, ROWS, KEYS), jnp.float32),
            pltpu.VMEM((2, ROWS, KEYS), jnp.bfloat16),
            pltpu.VMEM((2, ROWS, DIM), jnp.float32),
            pltpu.VMEM((2, ROWS, DIM), jnp.float32),
            pltpu.VMEM((ROWS, DIM), jnp.float32),
            pltpu.VMEM((ROWS, 2 * DIM), jnp.float32),
            pltpu.SemaphoreType.DMA((16,)),
        ],
    )(q, *pieces)
    soft = exchange(soft.reshape(NX * NZ, 8, HEADS * DIM), ("ctx_0", "head"))
    soft_out = soft.reshape(NX, NZ, 8, HEADS * DIM).swapaxes(1, 2).reshape(32, NZ * HEADS * DIM)

    (lin_out,) = call(lightning_kernel, [block], 7, 1 << 29)(
        lin_q, lin_k, lin_v, log_decay, lin_gain.reshape(1, -1), keep, got
    )
    return (lin_out, soft_out)


def solution(mesh):
    finer = Mesh(
        mesh.devices.reshape(NX, NY, NC, NZ), ("ctx_0", "ctx_1", "ctx_2", "head")
    )
    placed = (
        P(CTX, "head"),
        P(CTX, "head"),
        P(CTX, "head"),
        P("head", CTX),
        P("head"),
        P(CTX_HEAD, None),
        P(CTX_HEAD, None),
    )
    return jax.shard_map(
        both,
        mesh=finer,
        in_specs=placed,
        out_specs=(P(CTX, "head"), P(CTX_HEAD, None)),
        check_vma=False,
    )
```
